32 devices in a mesh: groups: 2 (over x), blocks: 16 (over z, y, core).
Axes of the slice: x: 2, y: 2, z: 4, core: 2. Of those that a mesh axis runs over, the one named last changes fastest.
Arguments:
- activations: float32 [2048, 2048], P('blocks', 'groups'), parts along dimension 1, may hold values from -180 to 180
- cotangent: float32 [2048, 2048], P('blocks', 'groups'), parts along dimension 1, may hold values from -6 to 6
- gain: float32 [2048], P('blocks'), may hold values from 0.5 to 1.5
- left_one: float32 [16, 128, 128], P('blocks'), may hold values from -0.5 to 0.5
- right_one: float32 [128, 16, 16], P('blocks'), may hold values from -1.5 to 1.5
- left_two: float32 [16, 128, 128], P('blocks'), may hold values from -0.5 to 0.5
- right_two: float32 [128, 16, 16], P('blocks'), may hold values from -1.5 to 1.5
Outputs:
- output: float32 [2048, 2048], P('blocks', 'groups'), parts along dimension 1
- input_gradient: float32 [2048, 2048], P('blocks', 'groups'), parts along dimension 1
- gain_gradient: float32 [4096], P(('groups', 'blocks')), parts along dimension 0
- grad_left_one: float32 [32, 128, 128], P(('groups', 'blocks')), parts along dimension 0
- grad_right_one: float32 [256, 16, 16], P(('groups', 'blocks')), parts along dimension 0
- grad_left_two: float32 [32, 128, 128], P(('groups', 'blocks')), parts along dimension 0
- grad_right_two: float32 [256, 16, 16], P(('groups', 'blocks')), parts along dimension 0
The draws below stay inside these ranges and needn't reach their ends.
There are 2 independent parts, one for each index of `groups`. The reference program is written for one: setup_inputs(seed, part) draws one part's arguments, and reference() takes and returns one part's arrays. A program takes and returns all parts, laid end to end along the dimension named above; an argument that names none is the same for every part. Nothing has to cross between parts.
All inputs are finite; a program needn't handle non-finite values.
Results may differ from the reference program's by a relative error of at most 0.0001.
Values sent between devices are 32-bit elements; how exact they have to be, the bound alone decides.
No kernel may reach another device: no remote copies, remote signals or barrier semaphores. Data moves between devices by JAX's collectives and lax.ppermute only.
A program may use at most 64 MiB of HBM per device.

```python
import math
import jax
import jax.numpy as jnp
from jax import lax

NB = 16
BS = 128
TOKENS = 1024
D = 2048


def draw_activations(key, part):
    first_key = jax.random.fold_in(jax.random.fold_in(key, 11), 0)
    position = (jnp.arange(D) // BS).astype(jnp.float32) / (NB - 1)
    base = jnp.clip(jax.random.normal(first_key, (D, TOKENS), jnp.float32), -4.0, 4.0)
    return base * (1.0 + 2.0 * position)[:, None]


def block_scale(own_key, dims, cuts, low, largest):
    level, own = 1.0, jax.random.fold_in(own_key, 6)
    for dim, shards_of in cuts:
        steps = jnp.exp(jax.random.uniform(jax.random.fold_in(own, dim), (shards_of,), jnp.float32, low / len(cuts), largest / len(cuts)))
        level = level * jnp.repeat(steps, dims[dim] // shards_of).reshape([-1 if axis == dim else 1 for axis in range(len(dims))])
    return level


def bell_draw(stream_key, dims, width, bound, cuts=(), kind=jnp.bfloat16):
    drawn = width * jax.random.normal(stream_key, dims, jnp.float32)
    if cuts:
        drawn = drawn * block_scale(stream_key, dims, cuts, -0.22, 0.18)
    return jnp.clip(drawn, -bound, bound).astype(kind)


def setup_inputs(seed: int = 0, part: int = 0) -> dict:
    key_of = jax.random.split(jax.random.key(seed), 8)
    part_splits = jax.random.split(jax.random.fold_in(key_of[7], part), 8)
    activations = draw_activations(jax.random.fold_in(jax.random.fold_in(key_of[7], part), 71), part)
    cotangent = bell_draw(part_splits[1], (D, TOKENS), 1.0, 6.0, ((0, 16),), jnp.float32)
    gain = jnp.clip(1.0 + 0.1 * jax.random.normal(key_of[2], (D,), jnp.float32), 0.5, 1.5)
    left_one = bell_draw(key_of[3], (NB, BS, BS), BS ** -0.5, 0.5, ((0, 16),), jnp.float32)
    right_one = bell_draw(key_of[4], (BS, NB, NB), NB ** -0.5, 1.5, ((0, 16),), jnp.float32)
    left_two = bell_draw(key_of[5], (NB, BS, BS), BS ** -0.5, 0.5, ((0, 16),), jnp.float32)
    right_two = bell_draw(key_of[6], (BS, NB, NB), NB ** -0.5, 1.5, ((0, 16),), jnp.float32)
    return {"activations": activations, "cotangent": cotangent, "gain": gain, "left_one": left_one, "right_one": right_one, "left_two": left_two, "right_two": right_two}


COEFF = math.sqrt(2.0 / math.pi)
EPSILON = 1e-05

def gelu_value(values):
    return 0.5 * values * (1.0 + jnp.tanh(COEFF * (values + 0.044715 * values * values * values)))

def monarch(values, left, right):
    stacked = values.reshape(NB, BS, -1)
    first = jnp.einsum('bij,bit->bjt', left, stacked, precision=lax.Precision.HIGHEST)
    second = jnp.einsum('jbk,bjt->jkt', right, first, precision=lax.Precision.HIGHEST)
    return second.reshape(NB * BS, -1)

def forward(activations, gain, left_one, right_one, left_two, right_two):
    meansq = lax.optimization_barrier(jnp.sum(activations * activations, axis=0)) / (NB * BS)
    inverse_root = lax.rsqrt(meansq + EPSILON)
    normed_rows = activations * inverse_root[None, :] * gain[:, None]
    pre = monarch(normed_rows, left_one, right_one)
    return activations + monarch(gelu_value(pre), left_two, right_two)

def reference(activations, cotangent, gain, left_one, right_one, left_two, right_two):
    output, pullback = jax.vjp(forward, activations, gain, left_one, right_one, left_two, right_two)
    grads = pullback(cotangent)
    factor_matrix = TOKENS ** (-0.5)
    return (output, grads[0], grads[1] * factor_matrix, grads[2] * factor_matrix, grads[3] * factor_matrix, grads[4] * factor_matrix, grads[5] * factor_matrix)
```

```python
import functools
import math

import jax
import jax.numpy as jnp
from jax import lax
from jax.experimental import pallas as pl
from jax.experimental.pallas import tpu as pltpu
from jax.sharding import PartitionSpec as P

COEFF = math.sqrt(2.0 / math.pi)
CUBIC = 0.044715
EPSILON = 1e-05
HIGH = lax.Precision.HIGHEST
SUB = 8
LANE = 128


def gelu_value(values):
    return 0.5 * values * (1.0 + jnp.tanh(COEFF * (values + CUBIC * values * values * values)))


def gelu_slope(values):
    tangent = jnp.tanh(COEFF * (values + CUBIC * values * values * values))
    return 0.5 * (1.0 + tangent) + 0.5 * values * (1.0 - tangent * tangent) * COEFF * (
        1.0 + 3.0 * CUBIC * values * values
    )


def monarch_forward(stacked, left, right):
    first = jnp.einsum("bij,bit->bjt", left, stacked, precision=HIGH)
    regrouped = lax.all_to_all(first, "blocks", split_axis=1, concat_axis=0, tiled=True)
    second = jnp.einsum("jbk,bjt->jkt", right, regrouped, precision=HIGH)
    return (second, regrouped)


def monarch_backward(grad_out, stacked, left, right, regrouped, factor_matrix):
    grad_right = jnp.einsum("bjt,jkt->jbk", regrouped, grad_out, precision=HIGH) * factor_matrix
    grad_mid = jnp.einsum("jbk,jkt->bjt", right, grad_out, precision=HIGH)
    piece = lax.all_to_all(grad_mid, "blocks", split_axis=0, concat_axis=1, tiled=True)
    grad_stacked = jnp.einsum("bij,bjt->bit", left, piece, precision=HIGH)
    grad_left = jnp.einsum("bit,bjt->bij", stacked, piece, precision=HIGH) * factor_matrix
    return (grad_stacked, grad_left, grad_right)


def local_plain(activations, cotangent, gain, left_one, right_one, left_two, right_two):
    features, tokens = activations.shape
    blocks_here, block_order = left_one.shape[:2]
    outer_here, block_count = right_one.shape[:2]
    feature_width = features * lax.axis_size("blocks")
    factor_matrix = tokens ** (-0.5)
    squares = lax.psum(jnp.sum(activations * activations, axis=0), "blocks")
    inverse_root = lax.rsqrt(squares / feature_width + EPSILON)[None, :]
    centered_input = activations * inverse_root
    normed_rows = centered_input * gain[:, None]
    normed_stacked = normed_rows.reshape(blocks_here, block_order, tokens)
    second_one, regrouped_one = monarch_forward(normed_stacked, left_one, right_one)
    pre = second_one.reshape(features, tokens)
    acted_stacked = gelu_value(pre).reshape(blocks_here, block_order, tokens)
    second_two, regrouped_two = monarch_forward(acted_stacked, left_two, right_two)
    output = activations + second_two.reshape(features, tokens)
    grad_acted, grad_left_two, grad_right_two = monarch_backward(
        cotangent.reshape(outer_here, block_count, tokens),
        acted_stacked, left_two, right_two, regrouped_two, factor_matrix,
    )
    grad_pre = grad_acted.reshape(features, tokens) * gelu_slope(pre)
    inner = lax.psum(jnp.sum(grad_pre * pre, axis=0), "blocks")
    normalized_gradient, grad_left_one, grad_right_one = monarch_backward(
        grad_pre.reshape(outer_here, block_count, tokens),
        normed_stacked, left_one, right_one, regrouped_one, factor_matrix,
    )
    normalized_gradient = normalized_gradient.reshape(features, tokens)
    input_gradient = cotangent + inverse_root * (
        gain[:, None] * normalized_gradient - centered_input * (inner / feature_width)[None, :]
    )
    gain_gradient = jnp.sum(normalized_gradient * centered_input, axis=1) * factor_matrix
    return (output, input_gradient, gain_gradient, grad_left_one, grad_right_one, grad_left_two, grad_right_two)


def matmul(a, b):
    return lax.dot_general(a, b, (((1,), (0,)), ((), ())), precision=HIGH, preferred_element_type=jnp.float32)


def matmul_nt(a, b):
    return lax.dot_general(a, b, (((1,), (1,)), ((), ())), precision=HIGH, preferred_element_type=jnp.float32)


def iota(shape, dim):
    return lax.broadcasted_iota(jnp.int32, shape, dim)


class Plan:
    def __init__(self, count, features, tokens):
        self.count, self.features, self.tokens = count, features, tokens
        bits = count.bit_length() - 1
        self.inner = 1 << ((bits + 1) // 2)
        self.outer = count // self.inner
        self.rows = features // count
        self.chunks = tokens // LANE
        self.block_tiles = self.rows // SUB * self.chunks
        self.sum_tiles = self.chunks // SUB
        self.factor = tokens ** (-0.5)
        self.width = features * count

    def fits(self):
        whole = self.count & (self.count - 1) == 0 and self.count > 1
        return whole and self.rows % SUB == 0 and self.rows > 0 and self.tokens % (SUB * LANE) == 0

    def message(self, blocks, sums):
        return jax.ShapeDtypeStruct((blocks * self.block_tiles + (self.sum_tiles if sums else 0), SUB, LANE), jnp.float32)

    def tiles(self):
        for r in range(self.rows // SUB):
            for c in range(self.chunks):
                yield r * self.chunks + c, r * SUB, c * LANE

    def put_block(self, source, block, message, slot):
        start = pl.multiple_of(block * self.rows, SUB)
        for i, r, c in self.tiles():
            message[slot * self.block_tiles + i] = source[pl.ds(start + r, SUB), c : c + LANE]

    def take_block(self, message, slot, target, block, scale=None):
        start = pl.multiple_of(block * self.rows, SUB)
        for i, r, c in self.tiles():
            tile = message[slot * self.block_tiles + i]
            target[pl.ds(start + r, SUB), c : c + LANE] = tile if scale is None else tile * scale[:, c : c + LANE]

    def move_block(self, message, slot, target, place):
        size = self.block_tiles
        target[place * size : (place + 1) * size] = message[slot * size : (slot + 1) * size]

    def put_sums(self, row, message, blocks):
        for s in range(self.sum_tiles):
            pieces = [row[:, (s * SUB + c) * LANE : (s * SUB + c + 1) * LANE] for c in range(SUB)]
            message[blocks * self.block_tiles + s] = jnp.concatenate(pieces, axis=0)

    def add_sums(self, messages, blocks):
        start = blocks * self.block_tiles
        return sum(message[start : start + self.sum_tiles] for message in messages)

    def sums_row(self, tiles):
        return jnp.concatenate([tiles[c // SUB, c % SUB : c % SUB + 1, :] for c in range(self.chunks)], axis=1)

    def call(self, kernel, outs, me, *args, scratch=(), flops=0):
        outs = tuple(o if isinstance(o, jax.ShapeDtypeStruct) else jax.ShapeDtypeStruct(o, jnp.float32) for o in outs)
        moved = 4 * sum(math.prod(a.shape) for a in (*args, *outs))
        vmem = pl.BlockSpec(memory_space=pltpu.VMEM)
        return pl.pallas_call(
            functools.partial(kernel, self, len(args), len(outs)),
            out_shape=outs,
            in_specs=[pl.BlockSpec(memory_space=pltpu.SMEM)] + [vmem] * len(args),
            out_specs=(vmem,) * len(outs),
            scratch_shapes=[pltpu.VMEM(s, jnp.float32) for s in scratch],
            cost_estimate=pl.CostEstimate(flops=flops, bytes_accessed=moved, transcendentals=0),
            name=kernel.__name__,
        )(me, *args)


def split_refs(n_in, n_out, refs):
    return refs[0], refs[1 : 1 + n_in], refs[1 + n_in : 1 + n_in + n_out], refs[1 + n_in + n_out :]


def first_one(plan, n_in, n_out, *refs):
    me, (x, left, gain), outs, (held,) = split_refs(n_in, n_out, refs)
    z, p = me[0] // plan.inner, me[0] % plan.inner
    values = x[...]
    held[...] = matmul(left[...].T * gain[...], values)
    squares = jnp.sum(values * values, axis=0, keepdims=True)
    for k in range(plan.outer):
        for m in range(plan.inner):
            plan.put_block(held, (z ^ k) * plan.inner + (p ^ m), outs[k], m)
        plan.put_sums(squares, outs[k], plan.inner)


def widen(plan, right):
    rows, count, full = plan.rows, plan.count, plan.features
    spread = (iota((count, full), 1) % count == iota((count, full), 0)).astype(jnp.float32)
    same = iota((full, full), 0) // count == iota((full, full), 1) // count
    tall = jnp.where(same, matmul(right, spread), 0.0)
    i, o = iota((full, full), 1), iota((full, full), 0)
    swap = (i == (o % rows) * count + o // rows).astype(jnp.float32)
    return matmul(swap, tall)


def narrow(plan, product):
    rows, count, full = plan.rows, plan.count, plan.features
    same = iota((full, full), 0) % rows == iota((full, full), 1) // count
    kept = jnp.where(same, product, 0.0)
    o, i = iota((full, full), 0), iota((full, full), 1)
    swap = (i == (o % count) * rows + o // count).astype(jnp.float32)
    gather = (iota((full, count), 0) % count == iota((full, count), 1)).astype(jnp.float32)
    return matmul(matmul(swap, kept), gather)


def back_two(plan, n_in, n_out, *refs):
    me, (cotangent, right_one, right_two), outs, (held,) = split_refs(n_in, n_out, refs)
    z, p = me[0] // plan.inner, me[0] % plan.inner
    wide_two = widen(plan, right_two[...])
    held[...] = matmul(wide_two, cotangent[...])
    for m in range(plan.inner):
        for k in range(plan.outer):
            plan.put_block(held, (z ^ k) * plan.inner + (p ^ m), outs[m], k)
    outs[-2][...] = widen(plan, right_one[...])
    outs[-1][...] = wide_two


def regroup(plan, n_in, n_out, *refs):
    _, ins, outs, _ = split_refs(n_in, n_out, refs)
    sums = ins[0].shape[0] > n_out * plan.block_tiles
    total = plan.add_sums(ins, n_out) if sums else None
    for o in range(n_out):
        for i in range(n_in):
            plan.move_block(ins[i], o, outs[o], i)
        if sums:
            outs[o][n_in * plan.block_tiles :] = total


def middle(plan, n_in, n_out, *refs):
    me, ins, outs, (y1, held) = split_refs(n_in, n_out, refs)
    z, p = me[0] // plan.inner, me[0] % plan.inner
    parts, (wide_one, left_two) = ins[: plan.inner], ins[plan.inner :]
    squares = plan.add_sums(parts, plan.outer)
    inverse_root = plan.sums_row(lax.rsqrt(squares / plan.width + EPSILON))
    for m in range(plan.inner):
        for k in range(plan.outer):
            plan.take_block(parts[m], k, y1, (z ^ k) * plan.inner + (p ^ m), inverse_root)
    first = y1[...]
    pre = matmul(wide_one[...].T, first)
    tangent = jnp.tanh(COEFF * (pre + CUBIC * pre * pre * pre))
    half = 0.5 * (1.0 + tangent)
    act = half * pre
    slope = half + 0.5 * pre * (1.0 - tangent * tangent) * COEFF * (1.0 + 3.0 * CUBIC * pre * pre)
    held[...] = matmul(left_two[...].T, act)
    for k in range(plan.outer):
        for m in range(plan.inner):
            plan.put_block(held, (z ^ k) * plan.inner + (p ^ m), outs[k], m)
    for ref, value in zip(outs[plan.outer :], (first, pre, act, slope, inverse_root)):
        ref[...] = value


def back_one(plan, n_in, n_out, *refs):
    me, ins, outs, (dy2, held) = split_refs(n_in, n_out, refs)
    z, p = me[0] // plan.inner, me[0] % plan.inner
    parts, (left_two, wide_one, pre, slope) = ins[: plan.outer], ins[plan.outer :]
    for k in range(plan.outer):
        for m in range(plan.inner):
            plan.take_block(parts[k], m, dy2, (z ^ k) * plan.inner + (p ^ m))
    back = dy2[...]
    dpre = matmul(left_two[...], back) * slope[...]
    inner = jnp.sum(dpre * pre[...], axis=0, keepdims=True)
    held[...] = matmul(wide_one[...], dpre)
    for m in range(plan.inner):
        for k in range(plan.outer):
            plan.put_block(held, (z ^ k) * plan.inner + (p ^ m), outs[m], k)
        plan.put_sums(inner, outs[m], plan.outer)
    outs[-2][...] = back
    outs[-1][...] = dpre


def grads_middle(plan, n_in, n_out, *refs):
    _, (y1, dpre, act, dy2), (grad_right_one, grad_left_two), _ = split_refs(n_in, n_out, refs)
    grad_right_one[...] = narrow(plan, matmul_nt(y1[...], dpre[...])) * plan.factor
    grad_left_two[...] = matmul_nt(act[...], dy2[...]) * plan.factor


def finish_output(plan, n_in, n_out, *refs):
    me, ins, (output, grad_right_two), (y2,) = split_refs(n_in, n_out, refs)
    z, p = me[0] // plan.inner, me[0] % plan.inner
    parts, (x, cotangent, wide_two) = ins[: plan.inner], ins[plan.inner :]
    for m in range(plan.inner):
        for k in range(plan.outer):
            plan.take_block(parts[m], k, y2, (z ^ k) * plan.inner + (p ^ m))
    second = y2[...]
    output[...] = x[...] + matmul(wide_two[...].T, second)
    grad_right_two[...] = narrow(plan, matmul_nt(second, cotangent[...])) * plan.factor


def finish_input(plan, n_in, n_out, *refs):
    me, ins, (input_gradient, gain_gradient, grad_left_one), (dy1,) = split_refs(n_in, n_out, refs)
    z, p = me[0] // plan.inner, me[0] % plan.inner
    parts, (x, cotangent, gain, left_one, inverse_root) = ins[: plan.outer], ins[plan.outer :]
    inner = plan.sums_row(plan.add_sums(parts, plan.inner)) / plan.width
    for k in range(plan.outer):
        for m in range(plan.inner):
            plan.take_block(parts[k], m, dy1, (z ^ k) * plan.inner + (p ^ m))
    back = dy1[...]
    root = inverse_root[...]
    xhat = x[...] * root
    turned = left_one[...].T
    scaled = matmul((turned * gain[...]).T, back)
    input_gradient[...] = cotangent[...] + root * (scaled - xhat * inner)
    product = matmul_nt(back, xhat)
    gain_gradient[...] = jnp.sum(turned * product, axis=0, keepdims=True) * plan.factor
    grad_left_one[...] = (product * gain[...] * plan.factor).T


def local_tiled(plan, activations, cotangent, gain, left_one, right_one, left_two, right_two):
    features, tokens, count = plan.features, plan.tokens, plan.count
    inner, outer = plan.inner, plan.outer
    me = lax.axis_index("blocks").astype(jnp.int32).reshape(1)
    full, square = (features, tokens), (features, features)
    cost = 12 * features * features * tokens

    def across(messages, step):
        moved = [
            lax.ppermute(message, "blocks", [(s, s ^ (i * step)) for s in range(count)])
            for i, message in enumerate(messages)
            if i
        ]
        return [messages[0], *moved]

    def over_outer(messages):
        return across(messages, inner)

    def over_inner(messages):
        return across(messages, 1)

    gain_row = gain.reshape(1, features)
    one, two = left_one.reshape(square), left_two.reshape(square)
    flat_one, flat_two = right_one.reshape(features, count), right_two.reshape(features, count)

    to_outer, to_inner = plan.message(inner, False), plan.message(outer, False)
    to_outer_sums, to_inner_sums = plan.message(inner, True), plan.message(outer, True)

    sent = plan.call(first_one, [to_outer_sums] * outer, me, activations, one, gain_row, scratch=[full], flops=cost)
    first_half = over_outer(sent)
    *sent, wide_one, wide_two = plan.call(
        back_two, [to_inner] * inner + [square] * 2, me, cotangent, flat_one, flat_two, scratch=[full], flops=cost
    )
    dy2_half = over_inner(sent)
    dy2_parts = over_outer(plan.call(regroup, [to_outer] * outer, me, *dy2_half))
    first_parts = over_inner(plan.call(regroup, [to_inner_sums] * inner, me, *first_half))
    *sent, y1, pre, act, slope, inverse_root = plan.call(
        middle, [to_outer] * outer + [full] * 4 + [(1, tokens)], me, *first_parts, wide_one, two, scratch=[full] * 2, flops=2 * cost
    )
    second_half = over_outer(sent)
    *sent, dy2, dpre = plan.call(
        back_one, [to_inner_sums] * inner + [full] * 2, me, *dy2_parts, two, wide_one, pre, slope, scratch=[full] * 2, flops=2 * cost
    )
    dy1_half = over_inner(sent)
    dy1_parts = over_outer(plan.call(regroup, [to_outer_sums] * outer, me, *dy1_half))
    grad_right_one, grad_left_two = plan.call(
        grads_middle, [(features, count), square], me, y1, dpre, act, dy2, flops=2 * cost
    )
    second_parts = over_inner(plan.call(regroup, [to_inner] * inner, me, *second_half))
    output, grad_right_two = plan.call(
        finish_output, [full, (features, count)], me, *second_parts, activations, cotangent, wide_two, scratch=[full], flops=2 * cost
    )
    input_gradient, gain_gradient, grad_left_one = plan.call(
        finish_input, [full, (1, features), square], me, *dy1_parts, activations, cotangent, gain_row, one, inverse_root,
        scratch=[full], flops=2 * cost,
    )
    return (
        output,
        input_gradient,
        gain_gradient.reshape(features),
        grad_left_one.reshape(left_one.shape),
        grad_right_one.reshape(right_one.shape),
        grad_left_two.reshape(left_two.shape),
        grad_right_two.reshape(right_two.shape),
    )


def local(activations, *rest):
    plan = Plan(lax.axis_size("blocks"), *activations.shape)
    if plan.fits() and rest[2].shape[0] == 1:
        return local_tiled(plan, activations, *rest)
    return local_plain(activations, *rest)


def solution(mesh):
    split = P("blocks", "groups")
    kept, laid = P("blocks", None, None), P(("groups", "blocks"), None, None)
    return jax.shard_map(
        local,
        mesh=mesh,
        in_specs=(split, split, P("blocks"), kept, kept, kept, kept),
        out_specs=(split, split, P(("groups", "blocks")), laid, laid, laid, laid),
        check_vma=False,
    )
```

```python
import functools
import math

import jax
import jax.numpy as jnp
from jax import lax
from jax.experimental import pallas as pl
from jax.experimental.pallas import tpu as pltpu
from jax.sharding import PartitionSpec as P

COEFF = math.sqrt(2.0 / math.pi)
CUBIC = 0.044715
EPSILON = 1e-05
HIGH = lax.Precision.HIGHEST
SUB = 8
LANE = 128
KERNEL_VMEM = 16 << 20


def gelu_value(values):
    return 0.5 * values * (1.0 + jnp.tanh(COEFF * (values + CUBIC * values * values * values)))


def gelu_slope(values):
    tangent = jnp.tanh(COEFF * (values + CUBIC * values * values * values))
    return 0.5 * (1.0 + tangent) + 0.5 * values * (1.0 - tangent * tangent) * COEFF * (
        1.0 + 3.0 * CUBIC * values * values
    )


def monarch_forward(stacked, left, right):
    first = jnp.einsum("bij,bit->bjt", left, stacked, precision=HIGH)
    regrouped = lax.all_to_all(first, "blocks", split_axis=1, concat_axis=0, tiled=True)
    second = jnp.einsum("jbk,bjt->jkt", right, regrouped, precision=HIGH)
    return (second, regrouped)


def monarch_backward(grad_out, stacked, left, right, regrouped, factor_matrix):
    grad_right = jnp.einsum("bjt,jkt->jbk", regrouped, grad_out, precision=HIGH) * factor_matrix
    grad_mid = jnp.einsum("jbk,jkt->bjt", right, grad_out, precision=HIGH)
    piece = lax.all_to_all(grad_mid, "blocks", split_axis=0, concat_axis=1, tiled=True)
    grad_stacked = jnp.einsum("bij,bjt->bit", left, piece, precision=HIGH)
    grad_left = jnp.einsum("bit,bjt->bij", stacked, piece, precision=HIGH) * factor_matrix
    return (grad_stacked, grad_left, grad_right)


def local_plain(activations, cotangent, gain, left_one, right_one, left_two, right_two):
    features, tokens = activations.shape
    blocks_here, block_order = left_one.shape[:2]
    outer_here, block_count = right_one.shape[:2]
    feature_width = features * lax.axis_size("blocks")
    factor_matrix = tokens ** (-0.5)
    squares = lax.psum(jnp.sum(activations * activations, axis=0), "blocks")
    inverse_root = lax.rsqrt(squares / feature_width + EPSILON)[None, :]
    centered_input = activations * inverse_root
    normed_rows = centered_input * gain[:, None]
    normed_stacked = normed_rows.reshape(blocks_here, block_order, tokens)
    second_one, regrouped_one = monarch_forward(normed_stacked, left_one, right_one)
    pre = second_one.reshape(features, tokens)
    acted_stacked = gelu_value(pre).reshape(blocks_here, block_order, tokens)
    second_two, regrouped_two = monarch_forward(acted_stacked, left_two, right_two)
    output = activations + second_two.reshape(features, tokens)
    grad_acted, grad_left_two, grad_right_two = monarch_backward(
        cotangent.reshape(outer_here, block_count, tokens),
        acted_stacked, left_two, right_two, regrouped_two, factor_matrix,
    )
    grad_pre = grad_acted.reshape(features, tokens) * gelu_slope(pre)
    inner = lax.psum(jnp.sum(grad_pre * pre, axis=0), "blocks")
    normalized_gradient, grad_left_one, grad_right_one = monarch_backward(
        grad_pre.reshape(outer_here, block_count, tokens),
        normed_stacked, left_one, right_one, regrouped_one, factor_matrix,
    )
    normalized_gradient = normalized_gradient.reshape(features, tokens)
    input_gradient = cotangent + inverse_root * (
        gain[:, None] * normalized_gradient - centered_input * (inner / feature_width)[None, :]
    )
    gain_gradient = jnp.sum(normalized_gradient * centered_input, axis=1) * factor_matrix
    return (output, input_gradient, gain_gradient, grad_left_one, grad_right_one, grad_left_two, grad_right_two)


def matmul(a, b):
    return lax.dot_general(a, b, (((1,), (0,)), ((), ())), precision=HIGH, preferred_element_type=jnp.float32)


def matmul_nt(a, b):
    return lax.dot_general(a, b, (((1,), (1,)), ((), ())), precision=HIGH, preferred_element_type=jnp.float32)


def iota(shape, dim):
    return lax.broadcasted_iota(jnp.int32, shape, dim)


class Plan:
    def __init__(self, count, features, tokens):
        self.count, self.features, self.tokens = count, features, tokens
        bits = count.bit_length() - 1
        self.inner = 1 << ((bits + 1) // 2)
        self.outer = count // self.inner
        self.rows = features // count
        self.chunks = tokens // LANE
        self.block_tiles = self.rows // SUB * self.chunks
        self.sum_tiles = self.chunks // SUB
        self.factor = tokens ** (-0.5)
        self.width = features * count

    def fits(self):
        whole = self.count & (self.count - 1) == 0 and self.count > 1
        return whole and self.rows % SUB == 0 and self.rows > 0 and self.tokens % (SUB * LANE) == 0

    def message(self, blocks, sums):
        return jax.ShapeDtypeStruct((blocks * self.block_tiles + (self.sum_tiles if sums else 0), SUB, LANE), jnp.float32)

    def tiles(self):
        for r in range(self.rows // SUB):
            for c in range(self.chunks):
                yield r * self.chunks + c, r * SUB, c * LANE

    def put_block(self, source, block, message, slot):
        start = pl.multiple_of(block * self.rows, SUB)
        for i, r, c in self.tiles():
            message[slot * self.block_tiles + i] = source[pl.ds(start + r, SUB), c : c + LANE]

    def take_block(self, message, slot, target, block, scale=None):
        start = pl.multiple_of(block * self.rows, SUB)
        for i, r, c in self.tiles():
            tile = message[slot * self.block_tiles + i]
            target[pl.ds(start + r, SUB), c : c + LANE] = tile if scale is None else tile * scale[:, c : c + LANE]

    def move_block(self, message, slot, target, place):
        size = self.block_tiles
        target[place * size : (place + 1) * size] = message[slot * size : (slot + 1) * size]

    def put_sums(self, row, message, blocks):
        for s in range(self.sum_tiles):
            pieces = [row[:, (s * SUB + c) * LANE : (s * SUB + c + 1) * LANE] for c in range(SUB)]
            message[blocks * self.block_tiles + s] = jnp.concatenate(pieces, axis=0)

    def add_sums(self, messages, blocks):
        start = blocks * self.block_tiles
        return sum(message[start : start + self.sum_tiles] for message in messages)

    def sums_row(self, tiles):
        return jnp.concatenate([tiles[c // SUB, c % SUB : c % SUB + 1, :] for c in range(self.chunks)], axis=1)

    def call(self, kernel, outs, me, *args, scratch=(), flops=0):
        outs = tuple(o if isinstance(o, jax.ShapeDtypeStruct) else jax.ShapeDtypeStruct(o, jnp.float32) for o in outs)
        moved = 4 * sum(math.prod(a.shape) for a in (*args, *outs))
        vmem = pl.BlockSpec(memory_space=pltpu.VMEM)
        return pl.pallas_call(
            functools.partial(kernel, self, len(args), len(outs)),
            out_shape=outs,
            in_specs=[pl.BlockSpec(memory_space=pltpu.SMEM)] + [vmem] * len(args),
            out_specs=(vmem,) * len(outs),
            scratch_shapes=[pltpu.VMEM(s, jnp.float32) for s in scratch],
            cost_estimate=pl.CostEstimate(flops=flops, bytes_accessed=moved, transcendentals=0),
            compiler_params=pltpu.CompilerParams(vmem_limit_bytes=KERNEL_VMEM),
            name=kernel.__name__,
        )(me, *args)


def split_refs(n_in, n_out, refs):
    return refs[0], refs[1 : 1 + n_in], refs[1 + n_in : 1 + n_in + n_out], refs[1 + n_in + n_out :]


def first_one(plan, n_in, n_out, *refs):
    me, (x, left, gain), outs, (held,) = split_refs(n_in, n_out, refs)
    z, p = me[0] // plan.inner, me[0] % plan.inner
    values = x[...]
    held[...] = matmul(left[...].T * gain[...], values)
    squares = jnp.sum(values * values, axis=0, keepdims=True)
    for k in range(plan.outer):
        for m in range(plan.inner):
            plan.put_block(held, (z ^ k) * plan.inner + (p ^ m), outs[k], m)
        plan.put_sums(squares, outs[k], plan.inner)


def widen(plan, right):
    rows, count, full = plan.rows, plan.count, plan.features
    spread = (iota((count, full), 1) % count == iota((count, full), 0)).astype(jnp.float32)
    same = iota((full, full), 0) // count == iota((full, full), 1) // count
    tall = jnp.where(same, matmul(right, spread), 0.0)
    i, o = iota((full, full), 1), iota((full, full), 0)
    swap = (i == (o % rows) * count + o // rows).astype(jnp.float32)
    return matmul(swap, tall)


def narrow(plan, product):
    rows, count, full = plan.rows, plan.count, plan.features
    same = iota((full, full), 0) % rows == iota((full, full), 1) // count
    kept = jnp.where(same, product, 0.0)
    o, i = iota((full, full), 0), iota((full, full), 1)
    swap = (i == (o % count) * rows + o // count).astype(jnp.float32)
    gather = (iota((full, count), 0) % count == iota((full, count), 1)).astype(jnp.float32)
    return matmul(matmul(swap, kept), gather)


def back_two(plan, n_in, n_out, *refs):
    me, (cotangent, right_one, right_two), outs, (held,) = split_refs(n_in, n_out, refs)
    z, p = me[0] // plan.inner, me[0] % plan.inner
    wide_two = widen(plan, right_two[...])
    held[...] = matmul(wide_two, cotangent[...])
    for m in range(plan.inner):
        for k in range(plan.outer):
            plan.put_block(held, (z ^ k) * plan.inner + (p ^ m), outs[m], k)
    outs[-2][...] = widen(plan, right_one[...])
    outs[-1][...] = wide_two


def regroup(plan, n_in, n_out, *refs):
    _, ins, outs, _ = split_refs(n_in, n_out, refs)
    sums = ins[0].shape[0] > n_out * plan.block_tiles
    total = plan.add_sums(ins, n_out) if sums else None
    for o in range(n_out):
        for i in range(n_in):
            plan.move_block(ins[i], o, outs[o], i)
        if sums:
            outs[o][n_in * plan.block_tiles :] = total


def middle(plan, n_in, n_out, *refs):
    me, ins, outs, (y1, held) = split_refs(n_in, n_out, refs)
    z, p = me[0] // plan.inner, me[0] % plan.inner
    parts, (wide_one, left_two) = ins[: plan.inner], ins[plan.inner :]
    squares = plan.add_sums(parts, plan.outer)
    inverse_root = plan.sums_row(lax.rsqrt(squares / plan.width + EPSILON))
    for m in range(plan.inner):
        for k in range(plan.outer):
            plan.take_block(parts[m], k, y1, (z ^ k) * plan.inner + (p ^ m), inverse_root)
    first = y1[...]
    pre = matmul(wide_one[...].T, first)
    tangent = jnp.tanh(COEFF * (pre + CUBIC * pre * pre * pre))
    half = 0.5 * (1.0 + tangent)
    act = half * pre
    slope = half + 0.5 * pre * (1.0 - tangent * tangent) * COEFF * (1.0 + 3.0 * CUBIC * pre * pre)
    held[...] = matmul(left_two[...].T, act)
    for k in range(plan.outer):
        for m in range(plan.inner):
            plan.put_block(held, (z ^ k) * plan.inner + (p ^ m), outs[k], m)
    for ref, value in zip(outs[plan.outer :], (first, pre, act, slope, inverse_root)):
        ref[...] = value


def back_one(plan, n_in, n_out, *refs):
    me, ins, outs, (dy2, held) = split_refs(n_in, n_out, refs)
    z, p = me[0] // plan.inner, me[0] % plan.inner
    parts, (left_two, wide_one, pre, slope) = ins[: plan.outer], ins[plan.outer :]
    for k in range(plan.outer):
        for m in range(plan.inner):
            plan.take_block(parts[k], m, dy2, (z ^ k) * plan.inner + (p ^ m))
    back = dy2[...]
    dpre = matmul(left_two[...], back) * slope[...]
    inner = jnp.sum(dpre * pre[...], axis=0, keepdims=True)
    held[...] = matmul(wide_one[...], dpre)
    for m in range(plan.inner):
        for k in range(plan.outer):
            plan.put_block(held, (z ^ k) * plan.inner + (p ^ m), outs[m], k)
        plan.put_sums(inner, outs[m], plan.outer)
    outs[-2][...] = back
    outs[-1][...] = dpre


def grads_middle(plan, n_in, n_out, *refs):
    _, (y1, dpre, act, dy2), (grad_right_one, grad_left_two), _ = split_refs(n_in, n_out, refs)
    grad_right_one[...] = narrow(plan, matmul_nt(y1[...], dpre[...])) * plan.factor
    grad_left_two[...] = matmul_nt(act[...], dy2[...]) * plan.factor


def finish_output(plan, n_in, n_out, *refs):
    me, ins, (output, grad_right_two), (y2,) = split_refs(n_in, n_out, refs)
    z, p = me[0] // plan.inner, me[0] % plan.inner
    parts, (x, cotangent, wide_two) = ins[: plan.inner], ins[plan.inner :]
    for m in range(plan.inner):
        for k in range(plan.outer):
            plan.take_block(parts[m], k, y2, (z ^ k) * plan.inner + (p ^ m))
    second = y2[...]
    output[...] = x[...] + matmul(wide_two[...].T, second)
    grad_right_two[...] = narrow(plan, matmul_nt(second, cotangent[...])) * plan.factor


def finish_input(plan, n_in, n_out, *refs):
    me, ins, (input_gradient, gain_gradient, grad_left_one), (dy1,) = split_refs(n_in, n_out, refs)
    z, p = me[0] // plan.inner, me[0] % plan.inner
    parts, (x, cotangent, gain, left_one, inverse_root) = ins[: plan.outer], ins[plan.outer :]
    inner = plan.sums_row(plan.add_sums(parts, plan.inner)) / plan.width
    for k in range(plan.outer):
        for m in range(plan.inner):
            plan.take_block(parts[k], m, dy1, (z ^ k) * plan.inner + (p ^ m))
    back = dy1[...]
    root = inverse_root[...]
    xhat = x[...] * root
    turned = left_one[...].T
    scaled = matmul((turned * gain[...]).T, back)
    input_gradient[...] = cotangent[...] + root * (scaled - xhat * inner)
    product = matmul_nt(back, xhat)
    gain_gradient[...] = jnp.sum(turned * product, axis=0, keepdims=True) * plan.factor
    grad_left_one[...] = (product * gain[...] * plan.factor).T


def local_tiled(plan, activations, cotangent, gain, left_one, right_one, left_two, right_two):
    features, tokens, count = plan.features, plan.tokens, plan.count
    inner, outer = plan.inner, plan.outer
    me = lax.axis_index("blocks").astype(jnp.int32).reshape(1)
    full, square = (features, tokens), (features, features)
    cost = 12 * features * features * tokens

    def across(messages, step):
        moved = [
            lax.ppermute(message, "blocks", [(s, s ^ (i * step)) for s in range(count)])
            for i, message in enumerate(messages)
            if i
        ]
        return [messages[0], *moved]

    def over_outer(messages):
        return across(messages, inner)

    def over_inner(messages):
        return across(messages, 1)

    gain_row = gain.reshape(1, features)
    one, two = left_one.reshape(square), left_two.reshape(square)
    flat_one, flat_two = right_one.reshape(features, count), right_two.reshape(features, count)

    to_outer, to_inner = plan.message(inner, False), plan.message(outer, False)
    to_outer_sums, to_inner_sums = plan.message(inner, True), plan.message(outer, True)

    sent = plan.call(first_one, [to_outer_sums] * outer, me, activations, one, gain_row, scratch=[full], flops=cost)
    first_half = over_outer(sent)
    *sent, wide_one, wide_two = plan.call(
        back_two, [to_inner] * inner + [square] * 2, me, cotangent, flat_one, flat_two, scratch=[full], flops=cost
    )
    dy2_half = over_inner(sent)
    dy2_parts = over_outer(plan.call(regroup, [to_outer] * outer, me, *dy2_half))
    first_parts = over_inner(plan.call(regroup, [to_inner_sums] * inner, me, *first_half))
    *sent, y1, pre, act, slope, inverse_root = plan.call(
        middle, [to_outer] * outer + [full] * 4 + [(1, tokens)], me, *first_parts, wide_one, two, scratch=[full] * 2, flops=2 * cost
    )
    second_half = over_outer(sent)
    *sent, dy2, dpre = plan.call(
        back_one, [to_inner_sums] * inner + [full] * 2, me, *dy2_parts, two, wide_one, pre, slope, scratch=[full] * 2, flops=2 * cost
    )
    dy1_half = over_inner(sent)
    dy1_parts = over_outer(plan.call(regroup, [to_outer_sums] * outer, me, *dy1_half))
    grad_right_one, grad_left_two = plan.call(
        grads_middle, [(features, count), square], me, y1, dpre, act, dy2, flops=2 * cost
    )
    second_parts = over_inner(plan.call(regroup, [to_inner] * inner, me, *second_half))
    output, grad_right_two = plan.call(
        finish_output, [full, (features, count)], me, *second_parts, activations, cotangent, wide_two, scratch=[full], flops=2 * cost
    )
    input_gradient, gain_gradient, grad_left_one = plan.call(
        finish_input, [full, (1, features), square], me, *dy1_parts, activations, cotangent, gain_row, one, inverse_root,
        scratch=[full], flops=2 * cost,
    )
    return (
        output,
        input_gradient,
        gain_gradient.reshape(features),
        grad_left_one.reshape(left_one.shape),
        grad_right_one.reshape(right_one.shape),
        grad_left_two.reshape(left_two.shape),
        grad_right_two.reshape(right_two.shape),
    )


def local(activations, *rest):
    plan = Plan(lax.axis_size("blocks"), *activations.shape)
    if plan.fits() and rest[2].shape[0] == 1:
        return local_tiled(plan, activations, *rest)
    return local_plain(activations, *rest)


def solution(mesh):
    split = P("blocks", "groups")
    kept, laid = P("blocks", None, None), P(("groups", "blocks"), None, None)
    return jax.shard_map(
        local,
        mesh=mesh,
        in_specs=(split, split, P("blocks"), kept, kept, kept, kept),
        out_specs=(split, split, P(("groups", "blocks")), laid, laid, laid, laid),
        check_vma=False,
    )
```

```python
import functools
import math

import jax
import jax.numpy as jnp
from jax import lax
from jax.experimental import pallas as pl
from jax.experimental.pallas import tpu as pltpu
from jax.sharding import PartitionSpec as P


COEFF = math.sqrt(2.0 / math.pi)
CUBIC = 0.044715
EPSILON = 1e-05
HIGH = lax.Precision.HIGHEST
SUB = 8
LANE = 128
KERNEL_VMEM = 16 << 20
LOADING_VMEM = 60 << 20


def gelu_value(values):
    return 0.5 * values * (1.0 + jnp.tanh(COEFF * (values + CUBIC * values * values * values)))


def gelu_slope(values):
    tangent = jnp.tanh(COEFF * (values + CUBIC * values * values * values))
    return 0.5 * (1.0 + tangent) + 0.5 * values * (1.0 - tangent * tangent) * COEFF * (
        1.0 + 3.0 * CUBIC * values * values
    )


def monarch_forward(stacked, left, right):
    first = jnp.einsum("bij,bit->bjt", left, stacked, precision=HIGH)
    regrouped = lax.all_to_all(first, "blocks", split_axis=1, concat_axis=0, tiled=True)
    second = jnp.einsum("jbk,bjt->jkt", right, regrouped, precision=HIGH)
    return (second, regrouped)


def monarch_backward(grad_out, stacked, left, right, regrouped, factor_matrix):
    grad_right = jnp.einsum("bjt,jkt->jbk", regrouped, grad_out, precision=HIGH) * factor_matrix
    grad_mid = jnp.einsum("jbk,jkt->bjt", right, grad_out, precision=HIGH)
    piece = lax.all_to_all(grad_mid, "blocks", split_axis=0, concat_axis=1, tiled=True)
    grad_stacked = jnp.einsum("bij,bjt->bit", left, piece, precision=HIGH)
    grad_left = jnp.einsum("bit,bjt->bij", stacked, piece, precision=HIGH) * factor_matrix
    return (grad_stacked, grad_left, grad_right)


def local_plain(activations, cotangent, gain, left_one, right_one, left_two, right_two):
    features, tokens = activations.shape
    blocks_here, block_order = left_one.shape[:2]
    outer_here, block_count = right_one.shape[:2]
    feature_width = features * lax.axis_size("blocks")
    factor_matrix = tokens ** (-0.5)
    squares = lax.psum(jnp.sum(activations * activations, axis=0), "blocks")
    inverse_root = lax.rsqrt(squares / feature_width + EPSILON)[None, :]
    centered_input = activations * inverse_root
    normed_rows = centered_input * gain[:, None]
    normed_stacked = normed_rows.reshape(blocks_here, block_order, tokens)
    second_one, regrouped_one = monarch_forward(normed_stacked, left_one, right_one)
    pre = second_one.reshape(features, tokens)
    acted_stacked = gelu_value(pre).reshape(blocks_here, block_order, tokens)
    second_two, regrouped_two = monarch_forward(acted_stacked, left_two, right_two)
    output = activations + second_two.reshape(features, tokens)
    grad_acted, grad_left_two, grad_right_two = monarch_backward(
        cotangent.reshape(outer_here, block_count, tokens),
        acted_stacked, left_two, right_two, regrouped_two, factor_matrix,
    )
    grad_pre = grad_acted.reshape(features, tokens) * gelu_slope(pre)
    inner = lax.psum(jnp.sum(grad_pre * pre, axis=0), "blocks")
    normalized_gradient, grad_left_one, grad_right_one = monarch_backward(
        grad_pre.reshape(outer_here, block_count, tokens),
        normed_stacked, left_one, right_one, regrouped_one, factor_matrix,
    )
    normalized_gradient = normalized_gradient.reshape(features, tokens)
    input_gradient = cotangent + inverse_root * (
        gain[:, None] * normalized_gradient - centered_input * (inner / feature_width)[None, :]
    )
    gain_gradient = jnp.sum(normalized_gradient * centered_input, axis=1) * factor_matrix
    return (output, input_gradient, gain_gradient, grad_left_one, grad_right_one, grad_left_two, grad_right_two)


def parts_of(values, count=2):
    parts = []
    for _ in range(count):
        parts.append(values.astype(jnp.bfloat16))
        values = values - parts[-1].astype(jnp.float32)
    return parts


def dot(a, b, dim_b):
    return lax.dot_general(a, b, (((1,), (dim_b,)), ((), ())), preferred_element_type=jnp.float32)


def matmul(a, b):
    (a_high, a_low), (b_high, b_low) = parts_of(a), parts_of(b)
    return dot(jnp.concatenate([a_high, a_high, a_low], axis=1), jnp.concatenate([b_high, b_low, b_high], axis=0), 0)


def matmul_nt(a, b):
    (a_high, a_low), (b_high, b_low) = parts_of(a), parts_of(b)
    both = dot(a_high, jnp.concatenate([b_high, b_low], axis=0), 1)
    return both[:, : b.shape[0]] + both[:, b.shape[0] :] + dot(a_low, b_high, 1)


def pick_rows(chosen, values):
    ones = chosen.astype(jnp.bfloat16)
    return sum(dot(ones, part, 0) for part in reversed(parts_of(values, 3)))


def pick_columns(values, chosen):
    ones = chosen.astype(jnp.bfloat16)
    return sum(dot(part, ones, 0) for part in reversed(parts_of(values, 3)))


def iota(shape, dim):
    return lax.broadcasted_iota(jnp.int32, shape, dim)


def stages(count):
    inner = 1 << (count.bit_length() // 2)
    return inner, count // inner


def send_order(count):
    return [*range(count // 2, count), *range(1, count // 2)]


def early_keys(count):
    keys = [0, *send_order(count)]
    return keys[: count // 2], keys[count // 2 :]


class Plan:
    def __init__(self, count, features, tokens):
        self.count, self.features, self.tokens = count, features, tokens
        self.inner, self.outer = stages(count)
        self.early, self.late = early_keys(self.outer)
        self.far, self.near = range(self.outer // 2, self.outer), range(self.outer // 2)
        self.rows = features // count
        self.chunks = tokens // LANE
        self.block_tiles = self.rows // SUB * self.chunks
        self.sum_tiles = self.chunks // SUB
        self.factor = tokens ** (-0.5)
        self.width = features * count

    def fits(self):
        whole = self.count & (self.count - 1) == 0 and self.count > 2
        return whole and self.rows % SUB == 0 and self.rows > 0 and self.tokens % (SUB * LANE) == 0

    def message(self, blocks, sums):
        return jax.ShapeDtypeStruct((blocks * self.block_tiles + (self.sum_tiles if sums else 0), SUB, LANE), jnp.float32)

    def tiles(self):
        for r in range(self.rows // SUB):
            for c in range(self.chunks):
                yield r * self.chunks + c, r * SUB, c * LANE

    def put_block(self, source, block, message, slot):
        start = pl.multiple_of(block * self.rows, SUB)
        for i, r, c in self.tiles():
            message[slot * self.block_tiles + i] = source[pl.ds(start + r, SUB), c : c + LANE]

    def take_block(self, message, slot, target, block, scale=None):
        start = pl.multiple_of(block * self.rows, SUB)
        for i, r, c in self.tiles():
            tile = message[slot * self.block_tiles + i]
            target[pl.ds(start + r, SUB), c : c + LANE] = tile if scale is None else tile * scale[:, c : c + LANE]

    def move_block(self, message, slot, target, place):
        size = self.block_tiles
        target[place * size : (place + 1) * size] = message[slot * size : (slot + 1) * size]

    def put_sums(self, row, message, blocks):
        for s in range(self.sum_tiles):
            pieces = [row[:, (s * SUB + c) * LANE : (s * SUB + c + 1) * LANE] for c in range(SUB)]
            message[blocks * self.block_tiles + s] = jnp.concatenate(pieces, axis=0)

    def has_sums(self, message):
        return message.shape[0] % self.block_tiles != 0

    def add_sums(self, messages):
        return sum(message[message.shape[0] - self.sum_tiles :] for message in messages if self.has_sums(message))

    def sums_row(self, tiles):
        return jnp.concatenate([tiles[c // SUB, c % SUB : c % SUB + 1, :] for c in range(self.chunks)], axis=1)

    def call(self, kernel, outs, me, *args, scratch=(), flops=0, loads=False, stores=0, **fixed):
        outs = tuple(o if isinstance(o, jax.ShapeDtypeStruct) else jax.ShapeDtypeStruct(o, jnp.float32) for o in outs)
        moved = 4 * sum(math.prod(a.shape) for a in (*args, *outs))
        vmem = pl.BlockSpec(memory_space=pltpu.VMEM)
        return pl.pallas_call(
            functools.partial(kernel, self, len(args), len(outs), **fixed),
            out_shape=outs,
            in_specs=[pl.BlockSpec(memory_space=pltpu.SMEM)]
            + [pl.BlockSpec(memory_space=pltpu.HBM) if loads else vmem] * len(args),
            out_specs=(pl.BlockSpec(memory_space=pl.ANY),) * stores + (vmem,) * (len(outs) - stores),
            scratch_shapes=[pltpu.VMEM(s, jnp.float32) for s in scratch]
            + ([pltpu.VMEM(a.shape, a.dtype) for a in args] + [pltpu.SemaphoreType.DMA((len(args),))] if loads else [])
            + ([pltpu.SemaphoreType.DMA((stores,))] if stores else []),
            cost_estimate=pl.CostEstimate(flops=flops, bytes_accessed=moved, transcendentals=0),
            compiler_params=pltpu.CompilerParams(vmem_limit_bytes=LOADING_VMEM if loads else KERNEL_VMEM),
        )(me, *args)


def split_refs(n_in, n_out, refs):
    return refs[0], refs[1 : 1 + n_in], refs[1 + n_in : 1 + n_in + n_out], refs[1 + n_in + n_out :]


def first_one(plan, n_in, n_out, *refs):
    me, sources, outs, (held, x, left, gain, arrived) = split_refs(n_in, n_out, refs)
    z, p = me[0] // plan.inner, me[0] % plan.inner
    loads = [pltpu.make_async_copy(s, t, arrived.at[i]) for i, (s, t) in enumerate(zip(sources, (x, left, gain)))]
    for load in loads:
        load.start()
    for load in loads:
        load.wait()
    values = x[...]
    held[...] = matmul(left[...].T * gain[...], values)
    squares = jnp.sum(values * values, axis=0, keepdims=True)
    for k in range(plan.outer):
        for m in range(plan.inner):
            plan.put_block(held, (z ^ k) * plan.inner + (p ^ m), outs[k], m)
        plan.put_sums(squares, outs[k], plan.inner)


def widen(plan, right):
    rows, count, full = plan.rows, plan.count, plan.features
    spread = (iota((count, full), 1) % count == iota((count, full), 0)).astype(jnp.float32)
    same = iota((full, full), 0) // count == iota((full, full), 1) // count
    tall = jnp.where(same, pick_columns(right, spread), 0.0)
    i, o = iota((full, full), 1), iota((full, full), 0)
    swap = (i == (o % rows) * count + o // rows).astype(jnp.float32)
    return pick_rows(swap, tall)


def narrow(plan, product):
    rows, count, full = plan.rows, plan.count, plan.features
    same = iota((full, full), 0) % rows == iota((full, full), 1) // count
    kept = jnp.where(same, product, 0.0)
    o, i = iota((full, full), 0), iota((full, full), 1)
    swap = (i == (o % count) * rows + o // count).astype(jnp.float32)
    gather = (iota((full, count), 0) % count == iota((full, count), 1)).astype(jnp.float32)
    return pick_columns(pick_rows(swap, kept), gather)


def back_two(plan, n_in, n_out, *refs):
    me, (cotangent, right_two), outs, (held,) = split_refs(n_in, n_out, refs)
    z, p = me[0] // plan.inner, me[0] % plan.inner
    wide_two = widen(plan, right_two[...])
    held[...] = matmul(wide_two, cotangent[...])
    for m in range(plan.inner):
        for k in range(plan.outer):
            plan.put_block(held, (z ^ k) * plan.inner + (p ^ m), outs[m], k)
    outs[-1][...] = wide_two


def widen_one(plan, n_in, n_out, *refs):
    _, (right, left, gain), (wide, turned, scaled, gain_kept), _ = split_refs(n_in, n_out, refs)
    wide[...] = widen(plan, right[...])
    turned[...] = left[...].T
    scaled[...] = (left[...].T * gain[...]).T
    gain_kept[...] = gain[...]


def regroup(plan, n_in, n_out, *refs, data):
    _, ins, outs, _ = split_refs(n_in, n_out, refs)
    sums = plan.has_sums(outs[0])
    total = plan.add_sums(ins) if sums else None
    for o in range(n_out):
        for i in range(data):
            plan.move_block(ins[i], o, outs[o], i)
        if sums:
            outs[o][data * plan.block_tiles :] = total


def middle(plan, n_in, n_out, *refs):
    me, ins, outs, (y1, held) = split_refs(n_in, n_out, refs)
    z, p = me[0] // plan.inner, me[0] % plan.inner
    parts, (wide_one, left_two) = ins[: 2 * plan.inner], ins[2 * plan.inner :]
    squares = plan.add_sums(parts)
    inverse_root = plan.sums_row(lax.rsqrt(squares / plan.width + EPSILON))
    for m in range(plan.inner):
        for message, keys in ((parts[m], plan.early), (parts[plan.inner + m], plan.late)):
            for slot, k in enumerate(keys):
                plan.take_block(message, slot, y1, (z ^ k) * plan.inner + (p ^ m), inverse_root)
    first = y1[...]
    pre = matmul(wide_one[...].T, first)
    tangent = jnp.tanh(COEFF * (pre + CUBIC * pre * pre * pre))
    half = 0.5 * (1.0 + tangent)
    act = half * pre
    slope = half + 0.5 * pre * (1.0 - tangent * tangent) * COEFF * (1.0 + 3.0 * CUBIC * pre * pre)
    held[...] = matmul(left_two[...].T, act)
    for k in range(plan.outer):
        for m in range(plan.inner):
            plan.put_block(held, (z ^ k) * plan.inner + (p ^ m), outs[k], m)
    for ref, value in zip(outs[plan.outer :], (first, pre, act, slope, inverse_root)):
        ref[...] = value


def back_one(plan, n_in, n_out, *refs):
    me, ins, outs, (dy2, held) = split_refs(n_in, n_out, refs)
    z, p = me[0] // plan.inner, me[0] % plan.inner
    parts, (left_two, wide_one, pre, slope) = ins[: plan.outer], ins[plan.outer :]
    for k in range(plan.outer):
        for m in range(plan.inner):
            plan.take_block(parts[k], m, dy2, (z ^ k) * plan.inner + (p ^ m))
    back = dy2[...]
    dpre = matmul(left_two[...], back) * slope[...]
    inner = jnp.sum(dpre * pre[...], axis=0, keepdims=True)
    held[...] = matmul(wide_one[...], dpre)
    for m in range(plan.inner):
        for message, keys in ((outs[m], plan.far), (outs[plan.inner + m], plan.near)):
            for slot, k in enumerate(keys):
                plan.put_block(held, (z ^ k) * plan.inner + (p ^ m), message, slot)
        plan.put_sums(inner, outs[m], len(plan.far))
    outs[-2][...] = back
    outs[-1][...] = dpre


def grads_middle(plan, n_in, n_out, *refs):
    _, (y1, dpre, act, dy2), (grad_right_one, grad_left_two), _ = split_refs(n_in, n_out, refs)
    grad_right_one[...] = narrow(plan, matmul_nt(y1[...], dpre[...])) * plan.factor
    grad_left_two[...] = matmul_nt(act[...], dy2[...]) * plan.factor


def finish_output(plan, n_in, n_out, *refs):
    me, ins, (output, grad_right_two), (y2,) = split_refs(n_in, n_out, refs)
    z, p = me[0] // plan.inner, me[0] % plan.inner
    parts, (x, cotangent, wide_two) = ins[: plan.inner], ins[plan.inner :]
    for m in range(plan.inner):
        for k in range(plan.outer):
            plan.take_block(parts[m], k, y2, (z ^ k) * plan.inner + (p ^ m))
    second = y2[...]
    output[...] = x[...] + matmul(wide_two[...].T, second)
    grad_right_two[...] = narrow(plan, matmul_nt(second, cotangent[...])) * plan.factor


def finish_input(plan, n_in, n_out, *refs):
    me, ins, (input_gradient, gain_gradient, grad_left_one), (dy1, result, done) = split_refs(n_in, n_out, refs)
    z, p = me[0] // plan.inner, me[0] % plan.inner
    parts, (x, cotangent, gain, turned, scaled, inverse_root) = ins[: plan.outer], ins[plan.outer :]
    inner = plan.sums_row(plan.add_sums(parts)) / plan.width
    for k in range(plan.outer):
        for m in range(plan.inner):
            plan.take_block(parts[k], m, dy1, (z ^ k) * plan.inner + (p ^ m))
    back = dy1[...]
    root = inverse_root[...]
    xhat = x[...] * root
    result[...] = cotangent[...] + root * (matmul(scaled[...], back) - xhat * inner)
    store = pltpu.make_async_copy(result, input_gradient, done.at[0])
    store.start()
    product = matmul_nt(back, xhat)
    gain_gradient[...] = jnp.sum(turned[...] * product, axis=0, keepdims=True) * plan.factor
    grad_left_one[...] = (product * gain[...] * plan.factor).T
    store.wait()


def local_tiled(plan, activations, cotangent, gain, left_one, right_one, left_two, right_two):
    features, tokens, count = plan.features, plan.tokens, plan.count
    inner, outer = plan.inner, plan.outer
    me = lax.axis_index("blocks").astype(jnp.int32).reshape(1)
    full, square = (features, tokens), (features, features)
    cost = 12 * features * features * tokens

    def across(messages, step):
        moved = dict(messages)
        for i in messages:
            if i:
                moved[i] = lax.ppermute(messages[i], "blocks", [(s, s ^ (i * step)) for s in range(count)])
        return moved

    def over_outer(keys, messages):
        return across(dict(zip(keys, messages, strict=True)), inner)

    def over_inner(messages):
        return [*across(dict(enumerate(messages)), 1).values()]

    def call(kernel, outs, *args, **options):
        return plan.call(kernel, outs, me, *args, **options)

    gain_row = gain.reshape(1, features)
    one, two = left_one.reshape(square), left_two.reshape(square)
    flat_one, flat_two = right_one.reshape(features, count), right_two.reshape(features, count)

    message, line = plan.message, range(outer)
    early, late, far, near = plan.early, plan.late, plan.far, plan.near

    sent = call(
        first_one, [message(inner, True)] * outer, activations, one, gain_row, scratch=[full], flops=cost, loads=True
    )
    first = over_outer(line, sent)
    *sent, wide_two = call(
        back_two, [message(outer, False)] * inner + [square], cotangent, flat_two, scratch=[full], flops=cost
    )
    dy2_half = over_inner(sent)
    wide_one, turned_one, scaled_one, gain_kept = call(
        widen_one, [square] * 3 + [(1, features)], flat_one, one, gain_row, flops=cost // 8
    )
    sent = call(regroup, [message(len(early), False)] * inner, *(first[k] for k in early), data=len(early))
    first_early = over_inner(sent)
    sent = call(regroup, [message(inner, False)] * outer, *dy2_half, data=inner)
    dy2_parts = over_outer(line, sent)
    sent = call(regroup, [message(len(late), True)] * inner, *(first[k] for k in (*late, *early)), data=len(late))
    first_late = over_inner(sent)
    *sent, y1, pre, act, slope, inverse_root = call(
        middle, [message(inner, False)] * outer + [full] * 4 + [(1, tokens)], *first_early, *first_late, wide_one, two,
        scratch=[full] * 2, flops=2 * cost,
    )
    second_half = over_outer(line, sent)
    *sent, dy2, dpre = call(
        back_one, [message(len(far), True)] * inner + [message(len(near), False)] * inner + [full] * 2,
        *(dy2_parts[k] for k in line), two, wide_one, pre, slope, scratch=[full] * 2, flops=2 * cost,
    )
    dy1_far, dy1_near = over_inner(sent[:inner]), over_inner(sent[inner:])
    sent = call(regroup, [message(inner, True)] * len(far), *dy1_far, data=inner)
    dy1_parts = over_outer(far, sent)
    sent = call(regroup, [message(inner, True)] * len(near), *dy1_near, *dy1_far, data=inner)
    dy1_parts |= over_outer(near, sent)
    sent = call(regroup, [message(outer, False)] * inner, *(second_half[k] for k in line), data=outer)
    second_parts = over_inner(sent)
    grad_right_one, grad_left_two = call(grads_middle, [(features, count), square], y1, dpre, act, dy2, flops=2 * cost)
    output, grad_right_two = call(
        finish_output, [full, (features, count)], *second_parts, activations, cotangent, wide_two,
        scratch=[full], flops=2 * cost,
    )
    input_gradient, gain_gradient, grad_left_one = call(
        finish_input, [full, (1, features), square], *(dy1_parts[k] for k in line), activations, cotangent,
        gain_kept, turned_one, scaled_one, inverse_root, scratch=[full] * 2, flops=2 * cost, stores=1,
    )
    return (
        output,
        input_gradient,
        gain_gradient.reshape(features),
        grad_left_one.reshape(left_one.shape),
        grad_right_one.reshape(right_one.shape),
        grad_left_two.reshape(left_two.shape),
        grad_right_two.reshape(right_two.shape),
    )


def local(activations, *rest):
    plan = Plan(lax.axis_size("blocks"), *activations.shape)
    if plan.fits() and rest[2].shape[0] == 1:
        return local_tiled(plan, activations, *rest)
    return local_plain(activations, *rest)


def solution(mesh):
    split = P("blocks", "groups")
    kept, laid = P("blocks", None, None), P(("groups", "blocks"), None, None)
    return jax.shard_map(
        local,
        mesh=mesh,
        in_specs=(split, split, P("blocks"), kept, kept, kept, kept),
        out_specs=(split, split, P(("groups", "blocks")), laid, laid, laid, laid),
        check_vma=False,
    )
```

```python
import functools
import math

import jax
import jax.numpy as jnp
from jax import lax
from jax.experimental import pallas as pl
from jax.experimental.pallas import tpu as pltpu
from jax.sharding import PartitionSpec as P


COEFF = math.sqrt(2.0 / math.pi)
CUBIC = 0.044715
EPSILON = 1e-05
HIGH = lax.Precision.HIGHEST
SUB = 8
LANE = 128
KERNEL_VMEM = 16 << 20


def gelu_value(values):
    return 0.5 * values * (1.0 + jnp.tanh(COEFF * (values + CUBIC * values * values * values)))


def gelu_slope(values):
    tangent = jnp.tanh(COEFF * (values + CUBIC * values * values * values))
    return 0.5 * (1.0 + tangent) + 0.5 * values * (1.0 - tangent * tangent) * COEFF * (
        1.0 + 3.0 * CUBIC * values * values
    )


def monarch_forward(stacked, left, right):
    first = jnp.einsum("bij,bit->bjt", left, stacked, precision=HIGH)
    regrouped = lax.all_to_all(first, "blocks", split_axis=1, concat_axis=0, tiled=True)
    second = jnp.einsum("jbk,bjt->jkt", right, regrouped, precision=HIGH)
    return (second, regrouped)


def monarch_backward(grad_out, stacked, left, right, regrouped, factor_matrix):
    grad_right = jnp.einsum("bjt,jkt->jbk", regrouped, grad_out, precision=HIGH) * factor_matrix
    grad_mid = jnp.einsum("jbk,jkt->bjt", right, grad_out, precision=HIGH)
    piece = lax.all_to_all(grad_mid, "blocks", split_axis=0, concat_axis=1, tiled=True)
    grad_stacked = jnp.einsum("bij,bjt->bit", left, piece, precision=HIGH)
    grad_left = jnp.einsum("bit,bjt->bij", stacked, piece, precision=HIGH) * factor_matrix
    return (grad_stacked, grad_left, grad_right)


def local_plain(activations, cotangent, gain, left_one, right_one, left_two, right_two):
    features, tokens = activations.shape
    blocks_here, block_order = left_one.shape[:2]
    outer_here, block_count = right_one.shape[:2]
    feature_width = features * lax.axis_size("blocks")
    factor_matrix = tokens ** (-0.5)
    squares = lax.psum(jnp.sum(activations * activations, axis=0), "blocks")
    inverse_root = lax.rsqrt(squares / feature_width + EPSILON)[None, :]
    centered_input = activations * inverse_root
    normed_rows = centered_input * gain[:, None]
    normed_stacked = normed_rows.reshape(blocks_here, block_order, tokens)
    second_one, regrouped_one = monarch_forward(normed_stacked, left_one, right_one)
    pre = second_one.reshape(features, tokens)
    acted_stacked = gelu_value(pre).reshape(blocks_here, block_order, tokens)
    second_two, regrouped_two = monarch_forward(acted_stacked, left_two, right_two)
    output = activations + second_two.reshape(features, tokens)
    grad_acted, grad_left_two, grad_right_two = monarch_backward(
        cotangent.reshape(outer_here, block_count, tokens),
        acted_stacked, left_two, right_two, regrouped_two, factor_matrix,
    )
    grad_pre = grad_acted.reshape(features, tokens) * gelu_slope(pre)
    inner = lax.psum(jnp.sum(grad_pre * pre, axis=0), "blocks")
    normalized_gradient, grad_left_one, grad_right_one = monarch_backward(
        grad_pre.reshape(outer_here, block_count, tokens),
        normed_stacked, left_one, right_one, regrouped_one, factor_matrix,
    )
    normalized_gradient = normalized_gradient.reshape(features, tokens)
    input_gradient = cotangent + inverse_root * (
        gain[:, None] * normalized_gradient - centered_input * (inner / feature_width)[None, :]
    )
    gain_gradient = jnp.sum(normalized_gradient * centered_input, axis=1) * factor_matrix
    return (output, input_gradient, gain_gradient, grad_left_one, grad_right_one, grad_left_two, grad_right_two)


def parts_of(values, count=2):
    parts = []
    for _ in range(count):
        parts.append(values.astype(jnp.bfloat16))
        values = values - parts[-1].astype(jnp.float32)
    return parts


def dot(a, b, dim_b):
    return lax.dot_general(a, b, (((1,), (dim_b,)), ((), ())), preferred_element_type=jnp.float32)


def matmul(a, b):
    (a_high, a_low), (b_high, b_low) = parts_of(a), parts_of(b)
    return dot(jnp.concatenate([a_high, a_high, a_low], axis=1), jnp.concatenate([b_high, b_low, b_high], axis=0), 0)


def matmul_nt(a, b):
    (a_high, a_low), (b_high, b_low) = parts_of(a), parts_of(b)
    both = dot(a_high, jnp.concatenate([b_high, b_low], axis=0), 1)
    return both[:, : b.shape[0]] + both[:, b.shape[0] :] + dot(a_low, b_high, 1)


def pair_of(values):
    return jnp.concatenate(parts_of(values), axis=0)


def stacked_left(rows):
    high, low = (part.astype(jnp.float32) for part in parts_of(rows))
    return jnp.concatenate([high, high, low, low], axis=0).T.astype(jnp.bfloat16)


def matmul_stacked(left, b):
    high, low = parts_of(b)
    return dot(left, jnp.concatenate([high, low, high, low], axis=0), 0)


def matmul_nt_pair(a, pair):
    both = dot(pair_of(a), pair, 1)
    rows, columns = a.shape[0], pair.shape[0] // 2
    both = both[:rows] + both[rows:]
    return both[:, :columns] + both[:, columns:]


def pick_rows(chosen, values):
    ones = chosen.astype(jnp.bfloat16)
    return sum(dot(ones, part, 0) for part in reversed(parts_of(values, 3)))


def pick_columns(values, chosen):
    ones = chosen.astype(jnp.bfloat16)
    return sum(dot(part, ones, 0) for part in reversed(parts_of(values, 3)))


def iota(shape, dim):
    return lax.broadcasted_iota(jnp.int32, shape, dim)


def stages(count):
    inner = 1 << (count.bit_length() // 2)
    return inner, count // inner


def send_order(count):
    return [*range(count // 2, count), *range(1, count // 2)]


def early_keys(count):
    keys = [0, *send_order(count)]
    return keys[: count // 2], keys[count // 2 :]


class Plan:
    def __init__(self, count, features, tokens):
        self.count, self.features, self.tokens = count, features, tokens
        self.inner, self.outer = stages(count)
        self.early, self.late = early_keys(self.outer)
        self.far, self.near = range(self.outer // 2, self.outer), range(self.outer // 2)
        self.rows = features // count
        self.chunks = tokens // LANE
        self.block_tiles = self.rows // SUB * self.chunks
        self.sum_tiles = self.chunks // SUB
        self.factor = tokens ** (-0.5)
        self.width = features * count

    def fits(self):
        whole = self.count & (self.count - 1) == 0 and self.count > 2
        return whole and self.rows % SUB == 0 and self.rows > 0 and self.tokens % (SUB * LANE) == 0

    def message(self, blocks, sums):
        return jax.ShapeDtypeStruct((blocks * self.block_tiles + (self.sum_tiles if sums else 0), SUB, LANE), jnp.float32)

    def tiles(self):
        for r in range(self.rows // SUB):
            for c in range(self.chunks):
                yield r * self.chunks + c, r * SUB, c * LANE

    def put_block(self, source, block, message, slot):
        start = pl.multiple_of(block * self.rows, SUB)
        for i, r, c in self.tiles():
            message[slot * self.block_tiles + i] = source[pl.ds(start + r, SUB), c : c + LANE]

    def take_block(self, message, slot, target, block, scale=None):
        start = pl.multiple_of(block * self.rows, SUB)
        for i, r, c in self.tiles():
            tile = message[slot * self.block_tiles + i]
            target[pl.ds(start + r, SUB), c : c + LANE] = tile if scale is None else tile * scale[:, c : c + LANE]

    def take_halves(self, parts, target, z, p, scale=None):
        for m in range(self.inner):
            for message, keys in ((parts[m], self.early), (parts[self.inner + m], self.late)):
                for slot, k in enumerate(keys):
                    self.take_block(message, slot, target, (z ^ k) * self.inner + (p ^ m), scale)

    def plane_spans(self, keys):
        return [(m, slot, k, m) for m in range(self.inner) for slot, k in enumerate(keys)]

    def line_spans(self, keys):
        return [(i, m, k, m) for i, k in enumerate(keys) for m in range(self.inner)]

    def line_up(self, parts, spans, target):
        for place, (i, slot, _, _) in enumerate(spans):
            for t, r, c in self.tiles():
                start = place * self.rows + r
                target[start : start + SUB, c : c + LANE] = parts[i][slot * self.block_tiles + t]

    def start_of(self, span, z, p):
        return pl.multiple_of(((z ^ span[2]) * self.inner + (p ^ span[3])) * self.rows, SUB)

    def gather_rows(self, table, spans, z, p):
        return jnp.concatenate([table[pl.ds(self.start_of(span, z, p), self.rows), :] for span in spans], axis=0)

    def scatter_rows(self, values, spans, target, z, p):
        for place, span in enumerate(spans):
            target[pl.ds(self.start_of(span, z, p), self.rows), :] = values[place * self.rows : (place + 1) * self.rows]

    def move_block(self, message, slot, target, place):
        size = self.block_tiles
        target[place * size : (place + 1) * size] = message[slot * size : (slot + 1) * size]

    def put_sums(self, row, message, blocks):
        for s in range(self.sum_tiles):
            pieces = [row[:, (s * SUB + c) * LANE : (s * SUB + c + 1) * LANE] for c in range(SUB)]
            message[blocks * self.block_tiles + s] = jnp.concatenate(pieces, axis=0)

    def has_sums(self, message):
        return message.shape[0] % self.block_tiles != 0

    def add_sums(self, messages):
        return sum(message[message.shape[0] - self.sum_tiles :] for message in messages if self.has_sums(message))

    def sums_row(self, tiles):
        return jnp.concatenate([tiles[c // SUB, c % SUB : c % SUB + 1, :] for c in range(self.chunks)], axis=1)

    def call(self, kernel, outs, me, *args, scratch=(), flops=0, loads=False, stores=0, **fixed):
        outs = tuple(o if isinstance(o, jax.ShapeDtypeStruct) else jax.ShapeDtypeStruct(o, jnp.float32) for o in outs)
        if loads:
            args = [pltpu.with_memory_space_constraint(a, pltpu.HBM) for a in args]
        moved = 4 * sum(math.prod(a.shape) for a in (*args, *outs))
        vmem = pl.BlockSpec(memory_space=pltpu.VMEM)
        return pl.pallas_call(
            functools.partial(kernel, self, len(args), len(outs), **fixed),
            out_shape=outs,
            in_specs=[pl.BlockSpec(memory_space=pltpu.SMEM)]
            + [pl.BlockSpec(memory_space=pltpu.HBM) if loads else vmem] * len(args),
            out_specs=(pl.BlockSpec(memory_space=pl.ANY),) * stores + (vmem,) * (len(outs) - stores),
            scratch_shapes=[pltpu.VMEM(s, jnp.float32) for s in scratch]
            + ([pltpu.VMEM(a.shape, a.dtype) for a in args] + [pltpu.SemaphoreType.DMA((len(args),))] if loads else [])
            + ([pltpu.SemaphoreType.DMA((stores,))] if stores else []),
            cost_estimate=pl.CostEstimate(flops=flops, bytes_accessed=moved, transcendentals=0),
            compiler_params=pltpu.CompilerParams(vmem_limit_bytes=KERNEL_VMEM),
        )(me, *args)


def split_refs(n_in, n_out, refs):
    return refs[0], refs[1 : 1 + n_in], refs[1 + n_in : 1 + n_in + n_out], refs[1 + n_in + n_out :]


def first_one(plan, n_in, n_out, *refs):
    me, sources, outs, (held, x, left, gain, arrived) = split_refs(n_in, n_out, refs)
    z, p = me[0] // plan.inner, me[0] % plan.inner
    loads = [pltpu.make_async_copy(s, t, arrived.at[i]) for i, (s, t) in enumerate(zip(sources, (x, left, gain)))]
    for load in loads:
        load.start()
    for load in loads:
        load.wait()
    values = x[...]
    held[...] = matmul(left[...].T * gain[...], values)
    squares = jnp.sum(values * values, axis=0, keepdims=True)
    for k in range(plan.outer):
        for m in range(plan.inner):
            plan.put_block(held, (z ^ k) * plan.inner + (p ^ m), outs[k], m)
        plan.put_sums(squares, outs[k], plan.inner)


def widen(plan, right):
    rows, count, full = plan.rows, plan.count, plan.features
    spread = (iota((count, full), 1) % count == iota((count, full), 0)).astype(jnp.float32)
    same = iota((full, full), 0) // count == iota((full, full), 1) // count
    tall = jnp.where(same, pick_columns(right, spread), 0.0)
    i, o = iota((full, full), 1), iota((full, full), 0)
    swap = (i == (o % rows) * count + o // rows).astype(jnp.float32)
    return pick_rows(swap, tall)


def narrow(plan, product):
    rows, count, full = plan.rows, plan.count, plan.features
    same = iota((full, full), 0) % rows == iota((full, full), 1) // count
    kept = jnp.where(same, product, 0.0)
    o, i = iota((full, full), 0), iota((full, full), 1)
    swap = (i == (o % count) * rows + o // count).astype(jnp.float32)
    gather = (iota((full, count), 0) % count == iota((full, count), 1)).astype(jnp.float32)
    return pick_columns(pick_rows(swap, kept), gather)


def back_two(plan, n_in, n_out, *refs):
    me, (cotangent, right_two), outs, (held,) = split_refs(n_in, n_out, refs)
    z, p = me[0] // plan.inner, me[0] % plan.inner
    wide_two = widen(plan, right_two[...])
    held[...] = matmul(wide_two, cotangent[...])
    for m in range(plan.inner):
        for k in range(plan.outer):
            plan.put_block(held, (z ^ k) * plan.inner + (p ^ m), outs[m], k)
    outs[-1][...] = wide_two


def prepare(plan, n_in, n_out, *refs):
    me, (right, left, gain, wide_two, x, cotangent), outs, (table,) = split_refs(n_in, n_out, refs)
    z, p = me[0] // plan.inner, me[0] % plan.inner
    wide, turned, gain_kept, scaled_early, scaled_late, wide_early, wide_late, x_pair, cotangent_pair = outs
    wide[...] = widen(plan, right[...])
    turned[...] = left[...].T
    gain_kept[...] = gain[...]
    table[...] = left[...].T * gain[...]
    scaled_early[...] = stacked_left(plan.gather_rows(table, plan.line_spans(plan.early), z, p))
    scaled_late[...] = stacked_left(plan.gather_rows(table, plan.line_spans(plan.late), z, p))
    wide_early[...] = stacked_left(plan.gather_rows(wide_two, plan.plane_spans(plan.early), z, p))
    wide_late[...] = stacked_left(plan.gather_rows(wide_two, plan.plane_spans(plan.late), z, p))
    x_pair[...] = pair_of(x[...])
    cotangent_pair[...] = pair_of(cotangent[...])


def regroup(plan, n_in, n_out, *refs, data):
    _, ins, outs, _ = split_refs(n_in, n_out, refs)
    sums = plan.has_sums(outs[0])
    total = plan.add_sums(ins) if sums else None
    for o in range(n_out):
        for i in range(data):
            plan.move_block(ins[i], o, outs[o], i)
        if sums:
            outs[o][data * plan.block_tiles :] = total


def middle(plan, n_in, n_out, *refs):
    me, ins, outs, (y1, held) = split_refs(n_in, n_out, refs)
    z, p = me[0] // plan.inner, me[0] % plan.inner
    parts, (wide_one, left_two) = ins[: 2 * plan.inner], ins[2 * plan.inner :]
    squares = plan.add_sums(parts)
    inverse_root = plan.sums_row(lax.rsqrt(squares / plan.width + EPSILON))
    plan.take_halves(parts, y1, z, p, inverse_root)
    first = y1[...]
    pre = matmul(wide_one[...].T, first)
    tangent = jnp.tanh(COEFF * (pre + CUBIC * pre * pre * pre))
    half = 0.5 * (1.0 + tangent)
    act = half * pre
    slope = half + 0.5 * pre * (1.0 - tangent * tangent) * COEFF * (1.0 + 3.0 * CUBIC * pre * pre)
    held[...] = matmul(left_two[...].T, act)
    for k in range(plan.outer):
        for m in range(plan.inner):
            plan.put_block(held, (z ^ k) * plan.inner + (p ^ m), outs[k], m)
    for ref, value in zip(outs[plan.outer :], (first, pre, act, slope, inverse_root)):
        ref[...] = value


def back_one(plan, n_in, n_out, *refs):
    me, ins, outs, (dy2, held) = split_refs(n_in, n_out, refs)
    z, p = me[0] // plan.inner, me[0] % plan.inner
    parts, (left_two, wide_one, pre, slope) = ins[: plan.outer], ins[plan.outer :]
    for k in range(plan.outer):
        for m in range(plan.inner):
            plan.take_block(parts[k], m, dy2, (z ^ k) * plan.inner + (p ^ m))
    back = dy2[...]
    dpre = matmul(left_two[...], back) * slope[...]
    inner = jnp.sum(dpre * pre[...], axis=0, keepdims=True)
    held[...] = matmul(wide_one[...], dpre)
    for m in range(plan.inner):
        for message, keys in ((outs[m], plan.far), (outs[plan.inner + m], plan.near)):
            for slot, k in enumerate(keys):
                plan.put_block(held, (z ^ k) * plan.inner + (p ^ m), message, slot)
        plan.put_sums(inner, outs[m], len(plan.far))
    outs[-2][...] = back
    outs[-1][...] = dpre


def grads_middle(plan, n_in, n_out, *refs):
    _, (y1, dpre, act, dy2), (grad_right_one, grad_left_two), _ = split_refs(n_in, n_out, refs)
    grad_right_one[...] = narrow(plan, matmul_nt(y1[...], dpre[...])) * plan.factor
    grad_left_two[...] = matmul_nt(act[...], dy2[...]) * plan.factor


def early_output(plan, n_in, n_out, *refs):
    _, ins, (partial, product), (y2,) = split_refs(n_in, n_out, refs)
    parts, (x, wide, cotangent_pair) = ins[: plan.inner], ins[plan.inner :]
    plan.line_up(parts, plan.plane_spans(plan.early), y2)
    second = y2[...]
    partial[...] = x[...] + matmul_stacked(wide[...], second)
    product[...] = matmul_nt_pair(second, cotangent_pair[...])


def finish_output(plan, n_in, n_out, *refs):
    me, ins, (output, grad_right_two), (y2, whole) = split_refs(n_in, n_out, refs)
    z, p = me[0] // plan.inner, me[0] % plan.inner
    parts, (partial, product, wide, cotangent_pair) = ins[: plan.inner], ins[plan.inner :]
    spans = plan.plane_spans(plan.late)
    plan.line_up(parts, spans, y2)
    second = y2[...]
    output[...] = partial[...] + matmul_stacked(wide[...], second)
    plan.scatter_rows(product[...], plan.plane_spans(plan.early), whole, z, p)
    plan.scatter_rows(matmul_nt_pair(second, cotangent_pair[...]), spans, whole, z, p)
    grad_right_two[...] = narrow(plan, whole[...]) * plan.factor


def early_input(plan, n_in, n_out, *refs):
    _, ins, (partial, product), (dy1,) = split_refs(n_in, n_out, refs)
    parts, (cotangent, scaled, x_pair, inverse_root) = ins[: len(plan.early)], ins[len(plan.early) :]
    plan.line_up(parts, plan.line_spans(plan.early), dy1)
    back = dy1[...] * inverse_root[...]
    partial[...] = cotangent[...] + matmul_stacked(scaled[...], back)
    product[...] = matmul_nt_pair(back, x_pair[...])


def finish_input(plan, n_in, n_out, *refs):
    me, ins, outs, (dy1, whole, *made, done) = split_refs(n_in, n_out, refs)
    z, p = me[0] // plan.inner, me[0] % plan.inner
    ready, parts, rest = ins[: n_out - len(made)], ins[n_out - len(made) :][: plan.outer], ins[n_out - len(made) + plan.outer :]
    x, x_pair, gain, turned, scaled, inverse_root, partial, product = rest
    stores = [pltpu.make_async_copy(s, t, done.at[i]) for i, (s, t) in enumerate(zip((*ready, *made), outs, strict=True))]
    for store in stores[: len(ready)]:
        store.start()
    input_gradient, gain_gradient, grad_left_one = made
    root = inverse_root[...]
    inner = plan.sums_row(plan.add_sums(parts)) / plan.width
    spans = plan.line_spans(plan.late)
    plan.line_up(parts[: len(plan.late)], spans, dy1)
    back = dy1[...] * root
    input_gradient[...] = partial[...] + matmul_stacked(scaled[...], back) - x[...] * (root * root * inner)
    stores[len(ready)].start()
    plan.scatter_rows(product[...], plan.line_spans(plan.early), whole, z, p)
    plan.scatter_rows(matmul_nt_pair(back, x_pair[...]), spans, whole, z, p)
    total = whole[...]
    gain_gradient[...] = jnp.sum(turned[...] * total, axis=0, keepdims=True) * plan.factor
    stores[len(ready) + 1].start()
    grad_left_one[...] = (total * gain[...] * plan.factor).T
    stores[len(ready) + 2].start()
    for store in stores:
        store.wait()


def local_tiled(plan, activations, cotangent, gain, left_one, right_one, left_two, right_two):
    features, tokens, count = plan.features, plan.tokens, plan.count
    inner, outer = plan.inner, plan.outer
    me = lax.axis_index("blocks").astype(jnp.int32).reshape(1)
    full, square = (features, tokens), (features, features)
    cost = 12 * features * features * tokens

    def across(messages, step):
        moved = dict(messages)
        for i in messages:
            if i:
                moved[i] = lax.ppermute(messages[i], "blocks", [(s, s ^ (i * step)) for s in range(count)])
        return moved

    def over_outer(keys, messages):
        return across(dict(zip(keys, messages, strict=True)), inner)

    def over_inner(messages):
        return [*across(dict(enumerate(messages)), 1).values()]

    def call(kernel, outs, *args, **options):
        return plan.call(kernel, outs, me, *args, **options)

    gain_row = gain.reshape(1, features)
    one, two = left_one.reshape(square), left_two.reshape(square)
    flat_one, flat_two = right_one.reshape(features, count), right_two.reshape(features, count)

    message, line = plan.message, range(outer)
    early, late, far, near = plan.early, plan.late, plan.far, plan.near

    sent = call(
        first_one, [message(inner, True)] * outer, activations, one, gain_row, scratch=[full], flops=cost, loads=True
    )
    first = over_outer(line, sent)
    *sent, wide_two = call(
        back_two, [message(outer, False)] * inner + [square], cotangent, flat_two, scratch=[full], flops=cost
    )
    dy2_half = over_inner(sent)
    half, stacked = (features // 2, tokens), jax.ShapeDtypeStruct((features, 2 * features), jnp.bfloat16)
    pair = jax.ShapeDtypeStruct((2 * features, tokens), jnp.bfloat16)
    wide_one, turned_one, gain_kept, scaled_early, scaled_late, wide_early, wide_late, x_pair, cotangent_pair = call(
        prepare, [square] * 2 + [(1, features)] + [stacked] * 4 + [pair] * 2,
        flat_one, one, gain_row, wide_two, activations, cotangent, scratch=[square], flops=cost // 8,
    )
    sent = call(regroup, [message(len(early), False)] * inner, *(first[k] for k in early), data=len(early))
    first_early = over_inner(sent)
    sent = call(regroup, [message(inner, False)] * outer, *dy2_half, data=inner)
    dy2_parts = over_outer(line, sent)
    sent = call(regroup, [message(len(late), True)] * inner, *(first[k] for k in (*late, *early)), data=len(late))
    first_late = over_inner(sent)
    *sent, y1, pre, act, slope, inverse_root = call(
        middle, [message(inner, False)] * outer + [full] * 4 + [(1, tokens)], *first_early, *first_late, wide_one, two,
        scratch=[full] * 2, flops=2 * cost,
    )
    second_half = over_outer(line, sent)
    *sent, dy2, dpre = call(
        back_one, [message(len(far), True)] * inner + [message(len(near), False)] * inner + [full] * 2,
        *(dy2_parts[k] for k in line), two, wide_one, pre, slope, scratch=[full] * 2, flops=2 * cost,
    )
    dy1_far, dy1_near = over_inner(sent[:inner]), over_inner(sent[inner:])
    sent = call(regroup, [message(inner, True)] * len(far), *dy1_far, data=inner)
    dy1_parts = over_outer(far, sent)
    sent = call(regroup, [message(inner, True)] * len(near), *dy1_near, *dy1_far, data=inner)
    dy1_parts |= over_outer(near, sent)
    sent = call(regroup, [message(len(early), False)] * inner, *(second_half[k] for k in early), data=len(early))
    second_early = over_inner(sent)
    sent = call(regroup, [message(len(late), False)] * inner, *(second_half[k] for k in late), data=len(late))
    second_late = over_inner(sent)
    grad_right_one, grad_left_two = call(grads_middle, [(features, count), square], y1, dpre, act, dy2, flops=2 * cost)
    partial_output, product_two = call(
        early_output, [full, (features // 2, features)], *second_early, activations, wide_early, cotangent_pair,
        scratch=[half], flops=cost,
    )
    partial_input, product_one = call(
        early_input, [full, (features // 2, features)], *(dy1_parts[k] for k in early), cotangent, scaled_early,
        x_pair, inverse_root, scratch=[half], flops=cost,
    )
    output, grad_right_two = call(
        finish_output, [full, (features, count)], *second_late, partial_output, product_two, wide_late,
        cotangent_pair, scratch=[half, square], flops=cost,
    )
    ready, made = [full, (features, count), square, (features, count)], [full, (1, features), square]
    output, grad_right_one, grad_left_two, grad_right_two, input_gradient, gain_gradient, grad_left_one = call(
        finish_input, ready + made, output, grad_right_one, grad_left_two, grad_right_two,
        *(dy1_parts[k] for k in (*late, *early)), activations, x_pair, gain_kept, turned_one, scaled_late, inverse_root,
        partial_input, product_one, scratch=[half, square, *made], flops=cost, stores=len(ready + made),
    )
    return (
        output,
        input_gradient,
        gain_gradient.reshape(features),
        grad_left_one.reshape(left_one.shape),
        grad_right_one.reshape(right_one.shape),
        grad_left_two.reshape(left_two.shape),
        grad_right_two.reshape(right_two.shape),
    )


def local(activations, *rest):
    plan = Plan(lax.axis_size("blocks"), *activations.shape)
    if plan.fits() and rest[2].shape[0] == 1:
        return local_tiled(plan, activations, *rest)
    return local_plain(activations, *rest)


def solution(mesh):
    split = P("blocks", "groups")
    kept, laid = P("blocks", None, None), P(("groups", "blocks"), None, None)
    return jax.shard_map(
        local,
        mesh=mesh,
        in_specs=(split, split, P("blocks"), kept, kept, kept, kept),
        out_specs=(split, split, P(("groups", "blocks")), laid, laid, laid, laid),
        check_vma=False,
    )
```

```python
import functools
import math

import jax
import jax.numpy as jnp
from jax import lax
from jax.experimental import pallas as pl
from jax.experimental.pallas import tpu as pltpu
from jax.sharding import PartitionSpec as P


COEFF = math.sqrt(2.0 / math.pi)
CUBIC = 0.044715
EPSILON = 1e-05
HIGH = lax.Precision.HIGHEST
SUB = 8
LANE = 128
KERNEL_VMEM = 16 << 20
LOADS = 1


def gelu_value(values):
    return 0.5 * values * (1.0 + jnp.tanh(COEFF * (values + CUBIC * values * values * values)))


def gelu_slope(values):
    tangent = jnp.tanh(COEFF * (values + CUBIC * values * values * values))
    return 0.5 * (1.0 + tangent) + 0.5 * values * (1.0 - tangent * tangent) * COEFF * (
        1.0 + 3.0 * CUBIC * values * values
    )


def monarch_forward(stacked, left, right):
    first = jnp.einsum("bij,bit->bjt", left, stacked, precision=HIGH)
    regrouped = lax.all_to_all(first, "blocks", split_axis=1, concat_axis=0, tiled=True)
    second = jnp.einsum("jbk,bjt->jkt", right, regrouped, precision=HIGH)
    return (second, regrouped)


def monarch_backward(grad_out, stacked, left, right, regrouped, factor_matrix):
    grad_right = jnp.einsum("bjt,jkt->jbk", regrouped, grad_out, precision=HIGH) * factor_matrix
    grad_mid = jnp.einsum("jbk,jkt->bjt", right, grad_out, precision=HIGH)
    piece = lax.all_to_all(grad_mid, "blocks", split_axis=0, concat_axis=1, tiled=True)
    grad_stacked = jnp.einsum("bij,bjt->bit", left, piece, precision=HIGH)
    grad_left = jnp.einsum("bit,bjt->bij", stacked, piece, precision=HIGH) * factor_matrix
    return (grad_stacked, grad_left, grad_right)


def local_plain(activations, cotangent, gain, left_one, right_one, left_two, right_two):
    features, tokens = activations.shape
    blocks_here, block_order = left_one.shape[:2]
    outer_here, block_count = right_one.shape[:2]
    feature_width = features * lax.axis_size("blocks")
    factor_matrix = tokens ** (-0.5)
    squares = lax.psum(jnp.sum(activations * activations, axis=0), "blocks")
    inverse_root = lax.rsqrt(squares / feature_width + EPSILON)[None, :]
    centered_input = activations * inverse_root
    normed_rows = centered_input * gain[:, None]
    normed_stacked = normed_rows.reshape(blocks_here, block_order, tokens)
    second_one, regrouped_one = monarch_forward(normed_stacked, left_one, right_one)
    pre = second_one.reshape(features, tokens)
    acted_stacked = gelu_value(pre).reshape(blocks_here, block_order, tokens)
    second_two, regrouped_two = monarch_forward(acted_stacked, left_two, right_two)
    output = activations + second_two.reshape(features, tokens)
    grad_acted, grad_left_two, grad_right_two = monarch_backward(
        cotangent.reshape(outer_here, block_count, tokens),
        acted_stacked, left_two, right_two, regrouped_two, factor_matrix,
    )
    grad_pre = grad_acted.reshape(features, tokens) * gelu_slope(pre)
    inner = lax.psum(jnp.sum(grad_pre * pre, axis=0), "blocks")
    normalized_gradient, grad_left_one, grad_right_one = monarch_backward(
        grad_pre.reshape(outer_here, block_count, tokens),
        normed_stacked, left_one, right_one, regrouped_one, factor_matrix,
    )
    normalized_gradient = normalized_gradient.reshape(features, tokens)
    input_gradient = cotangent + inverse_root * (
        gain[:, None] * normalized_gradient - centered_input * (inner / feature_width)[None, :]
    )
    gain_gradient = jnp.sum(normalized_gradient * centered_input, axis=1) * factor_matrix
    return (output, input_gradient, gain_gradient, grad_left_one, grad_right_one, grad_left_two, grad_right_two)


def parts_of(values, count=2):
    parts = []
    for _ in range(count):
        parts.append(values.astype(jnp.bfloat16))
        values = values - parts[-1].astype(jnp.float32)
    return parts


def dot(a, b, dim_b):
    return lax.dot_general(a, b, (((1,), (dim_b,)), ((), ())), preferred_element_type=jnp.float32)


def matmul(a, b):
    (a_high, a_low), (b_high, b_low) = parts_of(a), parts_of(b)
    return dot(jnp.concatenate([a_high, a_high, a_low], axis=1), jnp.concatenate([b_high, b_low, b_high], axis=0), 0)


def matmul_nt(a, b):
    (a_high, a_low), (b_high, b_low) = parts_of(a), parts_of(b)
    both = dot(a_high, jnp.concatenate([b_high, b_low], axis=0), 1)
    return both[:, : b.shape[0]] + both[:, b.shape[0] :] + dot(a_low, b_high, 1)


def pair_of(values):
    return jnp.concatenate(parts_of(values), axis=0)


def stacked_left(rows):
    high, low = (part.astype(jnp.float32) for part in parts_of(rows))
    return jnp.concatenate([high, high, low, low], axis=0).T.astype(jnp.bfloat16)


def matmul_stacked(left, b):
    high, low = parts_of(b)
    return dot(left, jnp.concatenate([high, low, high, low], axis=0), 0)


def matmul_nt_pair(a, pair):
    both = dot(pair_of(a), pair, 1)
    rows, columns = a.shape[0], pair.shape[0] // 2
    both = both[:rows] + both[rows:]
    return both[:, :columns] + both[:, columns:]


def pick_rows(chosen, values):
    ones = chosen.astype(jnp.bfloat16)
    return sum(dot(ones, part, 0) for part in reversed(parts_of(values, 3)))


def pick_columns(values, chosen):
    ones = chosen.astype(jnp.bfloat16)
    return sum(dot(part, ones, 0) for part in reversed(parts_of(values, 3)))


def iota(shape, dim):
    return lax.broadcasted_iota(jnp.int32, shape, dim)


def stages(count):
    inner = 1 << (count.bit_length() // 2)
    return inner, count // inner


def send_order(count):
    return [*range(count // 2, count), *range(1, count // 2)]


def early_keys(count):
    keys = [0, *send_order(count)]
    return keys[: count // 2], keys[count // 2 :]


def back_keys(count):
    places = send_order(count)
    return [places[0], *places[count // 2 :]], [*places[1 : count // 2], 0]


class Plan:
    def __init__(self, count, features, tokens):
        self.count, self.features, self.tokens = count, features, tokens
        self.inner, self.outer = stages(count)
        self.early, self.late = early_keys(self.outer)
        self.far, self.near = range(self.outer // 2, self.outer), range(self.outer // 2)
        self.sooner, self.later = back_keys(self.outer)
        self.rows = features // count
        self.chunks = tokens // LANE
        self.block_tiles = self.rows // SUB * self.chunks
        self.sum_tiles = self.chunks // SUB
        self.factor = tokens ** (-0.5)
        self.width = features * count

    def fits(self):
        whole = self.count & (self.count - 1) == 0 and self.count > 2
        return whole and self.rows % SUB == 0 and self.rows > 0 and self.tokens % (SUB * LANE) == 0

    def message(self, blocks, sums):
        return jax.ShapeDtypeStruct((blocks * self.block_tiles + (self.sum_tiles if sums else 0), SUB, LANE), jnp.float32)

    def tiles(self):
        for r in range(self.rows // SUB):
            for c in range(self.chunks):
                yield r * self.chunks + c, r * SUB, c * LANE

    def put_block(self, source, block, message, slot):
        start = pl.multiple_of(block * self.rows, SUB)
        for i, r, c in self.tiles():
            message[slot * self.block_tiles + i] = source[pl.ds(start + r, SUB), c : c + LANE]

    def take_block(self, message, slot, target, block, scale=None):
        start = pl.multiple_of(block * self.rows, SUB)
        for i, r, c in self.tiles():
            tile = message[slot * self.block_tiles + i]
            target[pl.ds(start + r, SUB), c : c + LANE] = tile if scale is None else tile * scale[:, c : c + LANE]

    def take_halves(self, parts, target, z, p, scale=None):
        for m in range(self.inner):
            for message, keys in ((parts[m], self.early), (parts[self.inner + m], self.late)):
                for slot, k in enumerate(keys):
                    self.take_block(message, slot, target, (z ^ k) * self.inner + (p ^ m), scale)

    def plane_spans(self, keys):
        return [(m, slot, k, m) for m in range(self.inner) for slot, k in enumerate(keys)]

    def line_spans(self, keys):
        return [(i, m, k, m) for i, k in enumerate(keys) for m in range(self.inner)]

    def sent_spans(self):
        return [(k, m, k, m) for k in range(self.outer) for m in range(self.inner)]

    def put_slots(self, values, messages, chunk):
        for place, (i, slot, _, _) in enumerate(self.sent_spans()):
            for r in range(self.rows // SUB):
                start = place * self.rows + r * SUB
                for c in range(values.shape[1] // LANE):
                    tile = slot * self.block_tiles + r * self.chunks + chunk + c
                    messages[i][tile] = values[start : start + SUB, c * LANE : (c + 1) * LANE]

    def line_up(self, parts, spans, target):
        for place, (i, slot, _, _) in enumerate(spans):
            for t, r, c in self.tiles():
                start = place * self.rows + r
                target[start : start + SUB, c : c + LANE] = parts[i][slot * self.block_tiles + t]

    def start_of(self, span, z, p):
        return pl.multiple_of(((z ^ span[2]) * self.inner + (p ^ span[3])) * self.rows, SUB)

    def gather_rows(self, table, spans, z, p):
        return jnp.concatenate([table[pl.ds(self.start_of(span, z, p), self.rows), :] for span in spans], axis=0)

    def scatter_rows(self, values, spans, target, z, p):
        for place, span in enumerate(spans):
            target[pl.ds(self.start_of(span, z, p), self.rows), :] = values[place * self.rows : (place + 1) * self.rows]

    def move_block(self, message, slot, target, place):
        size = self.block_tiles
        target[place * size : (place + 1) * size] = message[slot * size : (slot + 1) * size]

    def put_sums(self, row, message, blocks):
        for s in range(self.sum_tiles):
            pieces = [row[:, (s * SUB + c) * LANE : (s * SUB + c + 1) * LANE] for c in range(SUB)]
            message[blocks * self.block_tiles + s] = jnp.concatenate(pieces, axis=0)

    def has_sums(self, message):
        return message.shape[0] % self.block_tiles != 0

    def add_sums(self, messages):
        return sum(message[message.shape[0] - self.sum_tiles :] for message in messages if self.has_sums(message))

    def sums_row(self, tiles):
        return jnp.concatenate([tiles[c // SUB, c % SUB : c % SUB + 1, :] for c in range(self.chunks)], axis=1)

    def call(self, kernel, outs, me, *args, scratch=(), flops=0, loads=0, stores=0, **fixed):
        outs = tuple(o if isinstance(o, jax.ShapeDtypeStruct) else jax.ShapeDtypeStruct(o, jnp.float32) for o in outs)
        if loads:
            args = [pltpu.with_memory_space_constraint(a, pltpu.HBM) for a in args]
        moved = 4 * sum(math.prod(a.shape) for a in (*args, *outs))
        vmem = pl.BlockSpec(memory_space=pltpu.VMEM)
        return pl.pallas_call(
            functools.partial(kernel, self, len(args), len(outs), **fixed),
            out_shape=outs,
            in_specs=[pl.BlockSpec(memory_space=pltpu.SMEM)]
            + [pl.BlockSpec(memory_space=pltpu.HBM) if loads else vmem] * len(args),
            out_specs=(pl.BlockSpec(memory_space=pl.ANY),) * stores + (vmem,) * (len(outs) - stores),
            scratch_shapes=[pltpu.VMEM(s, jnp.float32) for s in scratch]
            + ([pltpu.VMEM(a.shape, a.dtype) for a in args] + [pltpu.SemaphoreType.DMA((loads,))] if loads else [])
            + ([pltpu.SemaphoreType.DMA((stores,))] if stores else []),
            cost_estimate=pl.CostEstimate(flops=flops, bytes_accessed=moved, transcendentals=0),
            compiler_params=pltpu.CompilerParams(vmem_limit_bytes=KERNEL_VMEM),
        )(me, *args)


def split_refs(n_in, n_out, refs):
    return refs[0], refs[1 : 1 + n_in], refs[1 + n_in : 1 + n_in + n_out], refs[1 + n_in + n_out :]


def first_one(plan, n_in, n_out, *refs):
    me, sources, outs, (turned, x, left, gain, arrived) = split_refs(n_in, n_out, refs)
    z, p = me[0] // plan.inner, me[0] % plan.inner
    width = plan.tokens // LOADS
    spans = [slice(i * width, (i + 1) * width) for i in range(LOADS)]
    loads = [pltpu.make_async_copy(s, t, arrived.at[i]) for i, (s, t) in enumerate(zip(sources[1:], (left, gain)))]
    loads += [pltpu.make_async_copy(sources[0].at[:, c], x.at[:, c], arrived.at[2 + i]) for i, c in enumerate(spans)]
    for load in loads:
        load.start()
    loads[0].wait()
    loads[1].wait()
    turned[...] = left[...].T * gain[...]
    weights = plan.gather_rows(turned, plan.sent_spans(), z, p)
    squares = []
    for i, c in enumerate(spans):
        loads[2 + i].wait()
        values = x[:, c]
        plan.put_slots(matmul(weights, values), outs, i * width // LANE)
        squares.append(jnp.sum(values * values, axis=0, keepdims=True))
    squares = jnp.concatenate(squares, axis=1)
    for out in outs:
        plan.put_sums(squares, out, plan.inner)


def widen(plan, right):
    rows, count, full = plan.rows, plan.count, plan.features
    spread = (iota((count, full), 1) % count == iota((count, full), 0)).astype(jnp.float32)
    same = iota((full, full), 0) // count == iota((full, full), 1) // count
    tall = jnp.where(same, pick_columns(right, spread), 0.0)
    i, o = iota((full, full), 1), iota((full, full), 0)
    swap = (i == (o % rows) * count + o // rows).astype(jnp.float32)
    return pick_rows(swap, tall)


def narrow(plan, product):
    rows, count, full = plan.rows, plan.count, plan.features
    same = iota((full, full), 0) % rows == iota((full, full), 1) // count
    kept = jnp.where(same, product, 0.0)
    o, i = iota((full, full), 0), iota((full, full), 1)
    swap = (i == (o % count) * rows + o // count).astype(jnp.float32)
    gather = (iota((full, count), 0) % count == iota((full, count), 1)).astype(jnp.float32)
    return pick_columns(pick_rows(swap, kept), gather)


def back_two(plan, n_in, n_out, *refs):
    me, (cotangent, right_two), outs, (held,) = split_refs(n_in, n_out, refs)
    z, p = me[0] // plan.inner, me[0] % plan.inner
    wide_two = widen(plan, right_two[...])
    held[...] = matmul(wide_two, cotangent[...])
    for m in range(plan.inner):
        for message, keys in ((outs[m], plan.far), (outs[plan.inner + m], plan.near)):
            for slot, k in enumerate(keys):
                plan.put_block(held, (z ^ k) * plan.inner + (p ^ m), message, slot)
    outs[-1][...] = wide_two


def prepare(plan, n_in, n_out, *refs):
    me, (right, left, gain, wide_two, x, cotangent), outs, (table,) = split_refs(n_in, n_out, refs)
    z, p = me[0] // plan.inner, me[0] % plan.inner
    wide, turned, gain_kept, scaled_early, scaled_late, wide_early, wide_late, x_pair, cotangent_pair = outs
    wide[...] = widen(plan, right[...])
    turned[...] = left[...].T
    gain_kept[...] = gain[...]
    table[...] = left[...].T * gain[...]
    scaled_early[...] = stacked_left(plan.gather_rows(table, plan.line_spans(plan.early), z, p))
    scaled_late[...] = stacked_left(plan.gather_rows(table, plan.line_spans(plan.late), z, p))
    wide_early[...] = stacked_left(plan.gather_rows(wide_two, plan.plane_spans(plan.early), z, p))
    wide_late[...] = stacked_left(plan.gather_rows(wide_two, plan.plane_spans(plan.late), z, p))
    x_pair[...] = pair_of(x[...])
    cotangent_pair[...] = pair_of(cotangent[...])


def regroup(plan, n_in, n_out, *refs, data):
    _, ins, outs, _ = split_refs(n_in, n_out, refs)
    sums = plan.has_sums(outs[0])
    total = plan.add_sums(ins) if sums else None
    for o in range(n_out):
        for i in range(data):
            plan.move_block(ins[i], o, outs[o], i)
        if sums:
            outs[o][data * plan.block_tiles :] = total


def middle(plan, n_in, n_out, *refs):
    me, ins, outs, (y1, held) = split_refs(n_in, n_out, refs)
    z, p = me[0] // plan.inner, me[0] % plan.inner
    parts, (wide_one, left_two) = ins[: 2 * plan.inner], ins[2 * plan.inner :]
    squares = plan.add_sums(parts)
    inverse_root = plan.sums_row(lax.rsqrt(squares / plan.width + EPSILON))
    plan.take_halves(parts, y1, z, p, inverse_root)
    first = y1[...]
    pre = matmul(wide_one[...].T, first)
    tangent = jnp.tanh(COEFF * (pre + CUBIC * pre * pre * pre))
    half = 0.5 * (1.0 + tangent)
    act = half * pre
    slope = half + 0.5 * pre * (1.0 - tangent * tangent) * COEFF * (1.0 + 3.0 * CUBIC * pre * pre)
    held[...] = matmul(left_two[...].T, act)
    for k in range(plan.outer):
        for m in range(plan.inner):
            plan.put_block(held, (z ^ k) * plan.inner + (p ^ m), outs[k], m)
    for ref, value in zip(outs[plan.outer :], (first, pre, act, slope, inverse_root)):
        ref[...] = value


def back_one(plan, n_in, n_out, *refs):
    me, ins, outs, (dy2, held) = split_refs(n_in, n_out, refs)
    z, p = me[0] // plan.inner, me[0] % plan.inner
    parts, (left_two, wide_one, pre, slope) = ins[: plan.outer], ins[plan.outer :]
    for k in range(plan.outer):
        for m in range(plan.inner):
            plan.take_block(parts[k], m, dy2, (z ^ k) * plan.inner + (p ^ m))
    back = dy2[...]
    dpre = matmul(left_two[...], back) * slope[...]
    inner = jnp.sum(dpre * pre[...], axis=0, keepdims=True)
    held[...] = matmul(wide_one[...], dpre)
    for m in range(plan.inner):
        for message, keys in ((outs[m], plan.sooner), (outs[plan.inner + m], plan.later)):
            for slot, k in enumerate(keys):
                plan.put_block(held, (z ^ k) * plan.inner + (p ^ m), message, slot)
        plan.put_sums(inner, outs[m], len(plan.sooner))
    outs[-2][...] = back
    outs[-1][...] = dpre


def grads_middle(plan, n_in, n_out, *refs):
    _, (y1, dpre, act, dy2), (grad_right_one, grad_left_two), _ = split_refs(n_in, n_out, refs)
    grad_right_one[...] = narrow(plan, matmul_nt(y1[...], dpre[...])) * plan.factor
    grad_left_two[...] = matmul_nt(act[...], dy2[...]) * plan.factor


def early_output(plan, n_in, n_out, *refs):
    _, ins, (partial, product), (y2,) = split_refs(n_in, n_out, refs)
    parts, (x, wide, cotangent_pair) = ins[: plan.inner], ins[plan.inner :]
    plan.line_up(parts, plan.plane_spans(plan.early), y2)
    second = y2[...]
    partial[...] = x[...] + matmul_stacked(wide[...], second)
    product[...] = matmul_nt_pair(second, cotangent_pair[...])


def finish_output(plan, n_in, n_out, *refs):
    me, ins, (output, grad_right_two), (y2, whole) = split_refs(n_in, n_out, refs)
    z, p = me[0] // plan.inner, me[0] % plan.inner
    parts, (partial, product, wide, cotangent_pair) = ins[: plan.inner], ins[plan.inner :]
    spans = plan.plane_spans(plan.late)
    plan.line_up(parts, spans, y2)
    second = y2[...]
    output[...] = partial[...] + matmul_stacked(wide[...], second)
    plan.scatter_rows(product[...], plan.plane_spans(plan.early), whole, z, p)
    plan.scatter_rows(matmul_nt_pair(second, cotangent_pair[...]), spans, whole, z, p)
    grad_right_two[...] = narrow(plan, whole[...]) * plan.factor


def early_input(plan, n_in, n_out, *refs):
    _, ins, (partial, product), (dy1,) = split_refs(n_in, n_out, refs)
    parts, (cotangent, scaled, x_pair, inverse_root) = ins[: len(plan.early)], ins[len(plan.early) :]
    plan.line_up(parts, plan.line_spans(plan.early), dy1)
    back = dy1[...] * inverse_root[...]
    partial[...] = cotangent[...] + matmul_stacked(scaled[...], back)
    product[...] = matmul_nt_pair(back, x_pair[...])


def finish_input(plan, n_in, n_out, *refs):
    me, ins, outs, (dy1, whole, *made, done) = split_refs(n_in, n_out, refs)
    z, p = me[0] // plan.inner, me[0] % plan.inner
    ready, parts, rest = ins[: n_out - len(made)], ins[n_out - len(made) :][: plan.outer], ins[n_out - len(made) + plan.outer :]
    x, x_pair, gain, turned, scaled, inverse_root, partial, product = rest
    stores = [pltpu.make_async_copy(s, t, done.at[i]) for i, (s, t) in enumerate(zip((*ready, *made), outs, strict=True))]
    for store in stores[: len(ready)]:
        store.start()
    input_gradient, gain_gradient, grad_left_one = made
    root = inverse_root[...]
    inner = plan.sums_row(plan.add_sums(parts)) / plan.width
    spans = plan.line_spans(plan.late)
    plan.line_up(parts[: len(plan.late)], spans, dy1)
    back = dy1[...] * root
    input_gradient[...] = partial[...] + matmul_stacked(scaled[...], back) - x[...] * (root * root * inner)
    stores[len(ready)].start()
    plan.scatter_rows(product[...], plan.line_spans(plan.early), whole, z, p)
    plan.scatter_rows(matmul_nt_pair(back, x_pair[...]), spans, whole, z, p)
    total = whole[...]
    gain_gradient[...] = jnp.sum(turned[...] * total, axis=0, keepdims=True) * plan.factor
    stores[len(ready) + 1].start()
    grad_left_one[...] = (total * gain[...] * plan.factor).T
    stores[len(ready) + 2].start()
    for store in stores:
        store.wait()


def local_tiled(plan, activations, cotangent, gain, left_one, right_one, left_two, right_two):
    features, tokens, count = plan.features, plan.tokens, plan.count
    inner, outer = plan.inner, plan.outer
    me = lax.axis_index("blocks").astype(jnp.int32).reshape(1)
    full, square = (features, tokens), (features, features)
    cost = 12 * features * features * tokens

    def across(messages, step):
        moved = dict(messages)
        for i in messages:
            if i:
                moved[i] = lax.ppermute(messages[i], "blocks", [(s, s ^ (i * step)) for s in range(count)])
        return moved

    def over_outer(keys, messages):
        return across(dict(zip(keys, messages, strict=True)), inner)

    def over_inner(messages):
        return [*across(dict(enumerate(messages)), 1).values()]

    def call(kernel, outs, *args, **options):
        return plan.call(kernel, outs, me, *args, **options)

    gain_row = gain.reshape(1, features)
    one, two = left_one.reshape(square), left_two.reshape(square)
    flat_one, flat_two = right_one.reshape(features, count), right_two.reshape(features, count)

    message, line = plan.message, range(outer)
    early, late, far, near = plan.early, plan.late, plan.far, plan.near

    sent = call(
        first_one, [message(inner, True)] * outer, activations, one, gain_row, scratch=[square], flops=cost, loads=LOADS + 2
    )
    first = over_outer(line, sent)
    *sent, wide_two = call(
        back_two, [message(len(far), False)] * inner + [message(len(near), False)] * inner + [square],
        cotangent, flat_two, scratch=[full], flops=cost,
    )
    dy2_far, dy2_near = over_inner(sent[:inner]), over_inner(sent[inner:])
    half, stacked = (features // 2, tokens), jax.ShapeDtypeStruct((features, 2 * features), jnp.bfloat16)
    pair = jax.ShapeDtypeStruct((2 * features, tokens), jnp.bfloat16)
    wide_one, turned_one, gain_kept, scaled_early, scaled_late, wide_early, wide_late, x_pair, cotangent_pair = call(
        prepare, [square] * 2 + [(1, features)] + [stacked] * 4 + [pair] * 2,
        flat_one, one, gain_row, wide_two, activations, cotangent, scratch=[square], flops=cost // 8,
    )
    sent = call(regroup, [message(len(early), False)] * inner, *(first[k] for k in early), data=len(early))
    first_early = over_inner(sent)
    sent = call(regroup, [message(inner, False)] * len(far), *dy2_far, data=inner)
    dy2_parts = over_outer(far, sent)
    sent = call(regroup, [message(inner, False)] * len(near), *dy2_near, data=inner)
    dy2_parts |= over_outer(near, sent)
    sent = call(regroup, [message(len(late), True)] * inner, *(first[k] for k in (*late, *early)), data=len(late))
    first_late = over_inner(sent)
    *sent, y1, pre, act, slope, inverse_root = call(
        middle, [message(inner, False)] * outer + [full] * 4 + [(1, tokens)], *first_early, *first_late, wide_one, two,
        scratch=[full] * 2, flops=2 * cost,
    )
    second_half = over_outer(line, sent)
    *sent, dy2, dpre = call(
        back_one, [message(len(plan.sooner), True)] * inner + [message(len(plan.later), False)] * inner + [full] * 2,
        *(dy2_parts[k] for k in line), two, wide_one, pre, slope, scratch=[full] * 2, flops=2 * cost,
    )
    dy1_sooner, dy1_later = over_inner(sent[:inner]), over_inner(sent[inner:])
    sent = call(regroup, [message(inner, True)] * len(plan.sooner), *dy1_sooner, data=inner)
    dy1_parts = over_outer(plan.sooner, sent)
    sent = call(regroup, [message(inner, True)] * len(plan.later), *dy1_later, *dy1_sooner, data=inner)
    dy1_parts |= over_outer(plan.later, sent)
    sent = call(regroup, [message(len(early), False)] * inner, *(second_half[k] for k in early), data=len(early))
    second_early = over_inner(sent)
    sent = call(regroup, [message(len(late), False)] * inner, *(second_half[k] for k in late), data=len(late))
    second_late = over_inner(sent)
    grad_right_one, grad_left_two = call(grads_middle, [(features, count), square], y1, dpre, act, dy2, flops=2 * cost)
    partial_output, product_two = call(
        early_output, [full, (features // 2, features)], *second_early, activations, wide_early, cotangent_pair,
        scratch=[half], flops=cost,
    )
    partial_input, product_one = call(
        early_input, [full, (features // 2, features)], *(dy1_parts[k] for k in early), cotangent, scaled_early,
        x_pair, inverse_root, scratch=[half], flops=cost,
    )
    output, grad_right_two = call(
        finish_output, [full, (features, count)], *second_late, partial_output, product_two, wide_late,
        cotangent_pair, scratch=[half, square], flops=cost,
    )
    ready, made = [full, (features, count), square, (features, count)], [full, (1, features), square]
    output, grad_right_one, grad_left_two, grad_right_two, input_gradient, gain_gradient, grad_left_one = call(
        finish_input, ready + made, output, grad_right_one, grad_left_two, grad_right_two,
        *(dy1_parts[k] for k in (*late, *early)), activations, x_pair, gain_kept, turned_one, scaled_late, inverse_root,
        partial_input, product_one, scratch=[half, square, *made], flops=cost, stores=len(ready + made),
    )
    return (
        output,
        input_gradient,
        gain_gradient.reshape(features),
        grad_left_one.reshape(left_one.shape),
        grad_right_one.reshape(right_one.shape),
        grad_left_two.reshape(left_two.shape),
        grad_right_two.reshape(right_two.shape),
    )


def local(activations, *rest):
    plan = Plan(lax.axis_size("blocks"), *activations.shape)
    if plan.fits() and rest[2].shape[0] == 1:
        return local_tiled(plan, activations, *rest)
    return local_plain(activations, *rest)


def solution(mesh):
    split = P("blocks", "groups")
    kept, laid = P("blocks", None, None), P(("groups", "blocks"), None, None)
    return jax.shard_map(
        local,
        mesh=mesh,
        in_specs=(split, split, P("blocks"), kept, kept, kept, kept),
        out_specs=(split, split, P(("groups", "blocks")), laid, laid, laid, laid),
        check_vma=False,
    )
```

```python
import functools
import math

import jax
import jax.numpy as jnp
from jax import lax
from jax.experimental import pallas as pl
from jax.experimental.pallas import tpu as pltpu
from jax.sharding import PartitionSpec as P


COEFF = math.sqrt(2.0 / math.pi)
CUBIC = 0.044715
EPSILON = 1e-05
HIGH = lax.Precision.HIGHEST
SUB = 8
LANE = 128
KERNEL_VMEM = 16 << 20
LOADS = 1


def gelu_value(values):
    return 0.5 * values * (1.0 + jnp.tanh(COEFF * (values + CUBIC * values * values * values)))


def gelu_slope(values):
    tangent = jnp.tanh(COEFF * (values + CUBIC * values * values * values))
    return 0.5 * (1.0 + tangent) + 0.5 * values * (1.0 - tangent * tangent) * COEFF * (
        1.0 + 3.0 * CUBIC * values * values
    )


def monarch_forward(stacked, left, right):
    first = jnp.einsum("bij,bit->bjt", left, stacked, precision=HIGH)
    regrouped = lax.all_to_all(first, "blocks", split_axis=1, concat_axis=0, tiled=True)
    second = jnp.einsum("jbk,bjt->jkt", right, regrouped, precision=HIGH)
    return (second, regrouped)


def monarch_backward(grad_out, stacked, left, right, regrouped, factor_matrix):
    grad_right = jnp.einsum("bjt,jkt->jbk", regrouped, grad_out, precision=HIGH) * factor_matrix
    grad_mid = jnp.einsum("jbk,jkt->bjt", right, grad_out, precision=HIGH)
    piece = lax.all_to_all(grad_mid, "blocks", split_axis=0, concat_axis=1, tiled=True)
    grad_stacked = jnp.einsum("bij,bjt->bit", left, piece, precision=HIGH)
    grad_left = jnp.einsum("bit,bjt->bij", stacked, piece, precision=HIGH) * factor_matrix
    return (grad_stacked, grad_left, grad_right)


def local_plain(activations, cotangent, gain, left_one, right_one, left_two, right_two):
    features, tokens = activations.shape
    blocks_here, block_order = left_one.shape[:2]
    outer_here, block_count = right_one.shape[:2]
    feature_width = features * lax.axis_size("blocks")
    factor_matrix = tokens ** (-0.5)
    squares = lax.psum(jnp.sum(activations * activations, axis=0), "blocks")
    inverse_root = lax.rsqrt(squares / feature_width + EPSILON)[None, :]
    centered_input = activations * inverse_root
    normed_rows = centered_input * gain[:, None]
    normed_stacked = normed_rows.reshape(blocks_here, block_order, tokens)
    second_one, regrouped_one = monarch_forward(normed_stacked, left_one, right_one)
    pre = second_one.reshape(features, tokens)
    acted_stacked = gelu_value(pre).reshape(blocks_here, block_order, tokens)
    second_two, regrouped_two = monarch_forward(acted_stacked, left_two, right_two)
    output = activations + second_two.reshape(features, tokens)
    grad_acted, grad_left_two, grad_right_two = monarch_backward(
        cotangent.reshape(outer_here, block_count, tokens),
        acted_stacked, left_two, right_two, regrouped_two, factor_matrix,
    )
    grad_pre = grad_acted.reshape(features, tokens) * gelu_slope(pre)
    inner = lax.psum(jnp.sum(grad_pre * pre, axis=0), "blocks")
    normalized_gradient, grad_left_one, grad_right_one = monarch_backward(
        grad_pre.reshape(outer_here, block_count, tokens),
        normed_stacked, left_one, right_one, regrouped_one, factor_matrix,
    )
    normalized_gradient = normalized_gradient.reshape(features, tokens)
    input_gradient = cotangent + inverse_root * (
        gain[:, None] * normalized_gradient - centered_input * (inner / feature_width)[None, :]
    )
    gain_gradient = jnp.sum(normalized_gradient * centered_input, axis=1) * factor_matrix
    return (output, input_gradient, gain_gradient, grad_left_one, grad_right_one, grad_left_two, grad_right_two)


def parts_of(values, count=2):
    parts = []
    for _ in range(count):
        parts.append(values.astype(jnp.bfloat16))
        values = values - parts[-1].astype(jnp.float32)
    return parts


def dot(a, b, dim_b):
    return lax.dot_general(a, b, (((1,), (dim_b,)), ((), ())), preferred_element_type=jnp.float32)


def matmul(a, b):
    (a_high, a_low), (b_high, b_low) = parts_of(a), parts_of(b)
    return dot(jnp.concatenate([a_high, a_high, a_low], axis=1), jnp.concatenate([b_high, b_low, b_high], axis=0), 0)


def matmul_nt(a, b):
    (a_high, a_low), (b_high, b_low) = parts_of(a), parts_of(b)
    both = dot(a_high, jnp.concatenate([b_high, b_low], axis=0), 1)
    return both[:, : b.shape[0]] + both[:, b.shape[0] :] + dot(a_low, b_high, 1)


def pair_of(values):
    return jnp.concatenate(parts_of(values), axis=0)


def stacked_left(rows):
    high, low = (part.astype(jnp.float32) for part in parts_of(rows))
    return jnp.concatenate([high, high, low, low], axis=0).T.astype(jnp.bfloat16)


def matmul_stacked(left, b):
    high, low = parts_of(b)
    return dot(left, jnp.concatenate([high, low, high, low], axis=0), 0)


def matmul_nt_pair(a, pair):
    both = dot(pair_of(a), pair, 1)
    rows, columns = a.shape[0], pair.shape[0] // 2
    both = both[:rows] + both[rows:]
    return both[:, :columns] + both[:, columns:]


def pick_rows(chosen, values):
    ones = chosen.astype(jnp.bfloat16)
    return sum(dot(ones, part, 0) for part in reversed(parts_of(values, 3)))


def pick_columns(values, chosen):
    ones = chosen.astype(jnp.bfloat16)
    return sum(dot(part, ones, 0) for part in reversed(parts_of(values, 3)))


def iota(shape, dim):
    return lax.broadcasted_iota(jnp.int32, shape, dim)


def stages(count):
    inner = 1 << (count.bit_length() // 2)
    return inner, count // inner


def send_order(count):
    return [*range(count // 2, count), *range(1, count // 2)]


def early_keys(count):
    keys = [0, *send_order(count)]
    return keys[: count // 2], keys[count // 2 :]


def back_keys(count):
    places = send_order(count)
    return [places[0], *places[count // 2 :]], [*places[1 : count // 2], 0]


class Plan:
    def __init__(self, count, features, tokens):
        self.count, self.features, self.tokens = count, features, tokens
        self.inner, self.outer = stages(count)
        self.early, self.late = early_keys(self.outer)
        self.far, self.near = range(self.outer // 2, self.outer), range(self.outer // 2)
        self.sooner, self.later = back_keys(self.outer)
        self.last = self.later[:1]
        self.soon = [k for k in range(self.outer) if k not in self.last]
        self.rows = features // count
        self.chunks = tokens // LANE
        self.block_tiles = self.rows // SUB * self.chunks
        self.sum_tiles = self.chunks // SUB
        self.factor = tokens ** (-0.5)
        self.width = features * count

    def fits(self):
        whole = self.count & (self.count - 1) == 0 and self.count > 2
        return whole and self.rows % SUB == 0 and self.rows > 0 and self.tokens % (SUB * LANE) == 0

    def message(self, blocks, sums):
        return jax.ShapeDtypeStruct((blocks * self.block_tiles + (self.sum_tiles if sums else 0), SUB, LANE), jnp.float32)

    def tiles(self):
        for r in range(self.rows // SUB):
            for c in range(self.chunks):
                yield r * self.chunks + c, r * SUB, c * LANE

    def put_block(self, source, block, message, slot):
        start = pl.multiple_of(block * self.rows, SUB)
        for i, r, c in self.tiles():
            message[slot * self.block_tiles + i] = source[pl.ds(start + r, SUB), c : c + LANE]

    def take_block(self, message, slot, target, block, scale=None):
        start = pl.multiple_of(block * self.rows, SUB)
        for i, r, c in self.tiles():
            tile = message[slot * self.block_tiles + i]
            target[pl.ds(start + r, SUB), c : c + LANE] = tile if scale is None else tile * scale[:, c : c + LANE]

    def take_halves(self, parts, target, z, p, scale=None):
        for m in range(self.inner):
            for message, keys in ((parts[m], self.early), (parts[self.inner + m], self.late)):
                for slot, k in enumerate(keys):
                    self.take_block(message, slot, target, (z ^ k) * self.inner + (p ^ m), scale)

    def plane_spans(self, keys):
        return [(m, slot, k, m) for m in range(self.inner) for slot, k in enumerate(keys)]

    def line_spans(self, keys):
        return [(i, m, k, m) for i, k in enumerate(keys) for m in range(self.inner)]

    def sent_spans(self):
        return [(k, m, k, m) for k in range(self.outer) for m in range(self.inner)]

    def put_slots(self, values, messages, chunk):
        for place, (i, slot, _, _) in enumerate(self.sent_spans()):
            for r in range(self.rows // SUB):
                start = place * self.rows + r * SUB
                for c in range(values.shape[1] // LANE):
                    tile = slot * self.block_tiles + r * self.chunks + chunk + c
                    messages[i][tile] = values[start : start + SUB, c * LANE : (c + 1) * LANE]

    def line_up(self, parts, spans, target):
        for place, (i, slot, _, _) in enumerate(spans):
            for t, r, c in self.tiles():
                start = place * self.rows + r
                target[start : start + SUB, c : c + LANE] = parts[i][slot * self.block_tiles + t]

    def start_of(self, span, z, p):
        return pl.multiple_of(((z ^ span[2]) * self.inner + (p ^ span[3])) * self.rows, SUB)

    def gather_rows(self, table, spans, z, p):
        return jnp.concatenate([table[pl.ds(self.start_of(span, z, p), self.rows), :] for span in spans], axis=0)

    def scatter_rows(self, values, spans, target, z, p):
        for place, span in enumerate(spans):
            target[pl.ds(self.start_of(span, z, p), self.rows), :] = values[place * self.rows : (place + 1) * self.rows]

    def move_block(self, message, slot, target, place):
        size = self.block_tiles
        target[place * size : (place + 1) * size] = message[slot * size : (slot + 1) * size]

    def put_sums(self, row, message, blocks):
        for s in range(self.sum_tiles):
            pieces = [row[:, (s * SUB + c) * LANE : (s * SUB + c + 1) * LANE] for c in range(SUB)]
            message[blocks * self.block_tiles + s] = jnp.concatenate(pieces, axis=0)

    def has_sums(self, message):
        return message.shape[0] % self.block_tiles != 0

    def add_sums(self, messages):
        return sum(message[message.shape[0] - self.sum_tiles :] for message in messages if self.has_sums(message))

    def sums_row(self, tiles):
        return jnp.concatenate([tiles[c // SUB, c % SUB : c % SUB + 1, :] for c in range(self.chunks)], axis=1)

    def call(self, kernel, outs, me, *args, scratch=(), flops=0, loads=0, stores=0, **fixed):
        outs = tuple(o if isinstance(o, jax.ShapeDtypeStruct) else jax.ShapeDtypeStruct(o, jnp.float32) for o in outs)
        if loads:
            args = [pltpu.with_memory_space_constraint(a, pltpu.HBM) for a in args]
        moved = 4 * sum(math.prod(a.shape) for a in (*args, *outs))
        vmem = pl.BlockSpec(memory_space=pltpu.VMEM)
        return pl.pallas_call(
            functools.partial(kernel, self, len(args), len(outs), **fixed),
            out_shape=outs,
            in_specs=[pl.BlockSpec(memory_space=pltpu.SMEM)]
            + [pl.BlockSpec(memory_space=pltpu.HBM) if loads else vmem] * len(args),
            out_specs=(pl.BlockSpec(memory_space=pl.ANY),) * stores + (vmem,) * (len(outs) - stores),
            scratch_shapes=[pltpu.VMEM(s, jnp.float32) for s in scratch]
            + ([pltpu.VMEM(a.shape, a.dtype) for a in args] + [pltpu.SemaphoreType.DMA((loads,))] if loads else [])
            + ([pltpu.SemaphoreType.DMA((stores,))] if stores else []),
            cost_estimate=pl.CostEstimate(flops=flops, bytes_accessed=moved, transcendentals=0),
            compiler_params=pltpu.CompilerParams(vmem_limit_bytes=KERNEL_VMEM),
        )(me, *args)


def split_refs(n_in, n_out, refs):
    return refs[0], refs[1 : 1 + n_in], refs[1 + n_in : 1 + n_in + n_out], refs[1 + n_in + n_out :]


def first_one(plan, n_in, n_out, *refs):
    me, sources, outs, (turned, x, left, gain, arrived) = split_refs(n_in, n_out, refs)
    z, p = me[0] // plan.inner, me[0] % plan.inner
    width = plan.tokens // LOADS
    spans = [slice(i * width, (i + 1) * width) for i in range(LOADS)]
    loads = [pltpu.make_async_copy(s, t, arrived.at[i]) for i, (s, t) in enumerate(zip(sources[1:], (left, gain)))]
    loads += [pltpu.make_async_copy(sources[0].at[:, c], x.at[:, c], arrived.at[2 + i]) for i, c in enumerate(spans)]
    for load in loads:
        load.start()
    loads[0].wait()
    loads[1].wait()
    turned[...] = left[...].T * gain[...]
    weights = plan.gather_rows(turned, plan.sent_spans(), z, p)
    squares = []
    for i, c in enumerate(spans):
        loads[2 + i].wait()
        values = x[:, c]
        plan.put_slots(matmul(weights, values), outs, i * width // LANE)
        squares.append(jnp.sum(values * values, axis=0, keepdims=True))
    squares = jnp.concatenate(squares, axis=1)
    for out in outs:
        plan.put_sums(squares, out, plan.inner)


def widen(plan, right):
    rows, count, full = plan.rows, plan.count, plan.features
    spread = (iota((count, full), 1) % count == iota((count, full), 0)).astype(jnp.float32)
    same = iota((full, full), 0) // count == iota((full, full), 1) // count
    tall = jnp.where(same, pick_columns(right, spread), 0.0)
    i, o = iota((full, full), 1), iota((full, full), 0)
    swap = (i == (o % rows) * count + o // rows).astype(jnp.float32)
    return pick_rows(swap, tall)


def narrow(plan, product):
    rows, count, full = plan.rows, plan.count, plan.features
    same = iota((full, full), 0) % rows == iota((full, full), 1) // count
    kept = jnp.where(same, product, 0.0)
    o, i = iota((full, full), 0), iota((full, full), 1)
    swap = (i == (o % count) * rows + o // count).astype(jnp.float32)
    gather = (iota((full, count), 0) % count == iota((full, count), 1)).astype(jnp.float32)
    return pick_columns(pick_rows(swap, kept), gather)


def back_two(plan, n_in, n_out, *refs):
    me, (cotangent, right_two), outs, (held,) = split_refs(n_in, n_out, refs)
    z, p = me[0] // plan.inner, me[0] % plan.inner
    wide_two = widen(plan, right_two[...])
    held[...] = matmul(wide_two, cotangent[...])
    for m in range(plan.inner):
        for message, keys in ((outs[m], plan.far), (outs[plan.inner + m], plan.near)):
            for slot, k in enumerate(keys):
                plan.put_block(held, (z ^ k) * plan.inner + (p ^ m), message, slot)
    outs[-1][...] = wide_two


def prepare(plan, n_in, n_out, *refs):
    me, (right, left, gain, wide_two, x, cotangent), outs, (table,) = split_refs(n_in, n_out, refs)
    z, p = me[0] // plan.inner, me[0] % plan.inner
    wide, turned, gain_kept, scaled_early, scaled_late, wide_early, wide_late, x_pair, cotangent_pair = outs
    wide[...] = widen(plan, right[...])
    turned[...] = left[...].T
    gain_kept[...] = gain[...]
    table[...] = left[...].T * gain[...]
    scaled_early[...] = stacked_left(plan.gather_rows(table, plan.line_spans(plan.soon), z, p))
    scaled_late[...] = stacked_left(plan.gather_rows(table, plan.line_spans(plan.last), z, p))
    wide_early[...] = stacked_left(plan.gather_rows(wide_two, plan.plane_spans(plan.early), z, p))
    wide_late[...] = stacked_left(plan.gather_rows(wide_two, plan.plane_spans(plan.late), z, p))
    x_pair[...] = pair_of(x[...])
    cotangent_pair[...] = pair_of(cotangent[...])


def regroup(plan, n_in, n_out, *refs, data):
    _, ins, outs, _ = split_refs(n_in, n_out, refs)
    sums = plan.has_sums(outs[0])
    total = plan.add_sums(ins) if sums else None
    for o in range(n_out):
        for i in range(data):
            plan.move_block(ins[i], o, outs[o], i)
        if sums:
            outs[o][data * plan.block_tiles :] = total


def middle(plan, n_in, n_out, *refs):
    me, ins, outs, (y1, held) = split_refs(n_in, n_out, refs)
    z, p = me[0] // plan.inner, me[0] % plan.inner
    parts, (wide_one, left_two) = ins[: 2 * plan.inner], ins[2 * plan.inner :]
    squares = plan.add_sums(parts)
    inverse_root = plan.sums_row(lax.rsqrt(squares / plan.width + EPSILON))
    plan.take_halves(parts, y1, z, p, inverse_root)
    first = y1[...]
    pre = matmul(wide_one[...].T, first)
    tangent = jnp.tanh(COEFF * (pre + CUBIC * pre * pre * pre))
    half = 0.5 * (1.0 + tangent)
    act = half * pre
    slope = half + 0.5 * pre * (1.0 - tangent * tangent) * COEFF * (1.0 + 3.0 * CUBIC * pre * pre)
    held[...] = matmul(left_two[...].T, act)
    for k in range(plan.outer):
        for m in range(plan.inner):
            plan.put_block(held, (z ^ k) * plan.inner + (p ^ m), outs[k], m)
    for ref, value in zip(outs[plan.outer :], (first, pre, act, slope, inverse_root)):
        ref[...] = value


def back_one(plan, n_in, n_out, *refs):
    me, ins, outs, (dy2, held) = split_refs(n_in, n_out, refs)
    z, p = me[0] // plan.inner, me[0] % plan.inner
    parts, (left_two, wide_one, pre, slope) = ins[: plan.outer], ins[plan.outer :]
    for k in range(plan.outer):
        for m in range(plan.inner):
            plan.take_block(parts[k], m, dy2, (z ^ k) * plan.inner + (p ^ m))
    back = dy2[...]
    dpre = matmul(left_two[...], back) * slope[...]
    inner = jnp.sum(dpre * pre[...], axis=0, keepdims=True)
    held[...] = matmul(wide_one[...], dpre)
    for m in range(plan.inner):
        for message, keys in ((outs[m], plan.sooner), (outs[plan.inner + m], plan.later)):
            for slot, k in enumerate(keys):
                plan.put_block(held, (z ^ k) * plan.inner + (p ^ m), message, slot)
        plan.put_sums(inner, outs[m], len(plan.sooner))
    outs[-2][...] = back
    outs[-1][...] = dpre


def grads_middle(plan, n_in, n_out, *refs):
    _, (y1, dpre, act, dy2), (grad_right_one, grad_left_two), _ = split_refs(n_in, n_out, refs)
    grad_right_one[...] = narrow(plan, matmul_nt(y1[...], dpre[...])) * plan.factor
    grad_left_two[...] = matmul_nt(act[...], dy2[...]) * plan.factor


def early_output(plan, n_in, n_out, *refs):
    _, ins, (partial, product), (y2,) = split_refs(n_in, n_out, refs)
    parts, (x, wide, cotangent_pair) = ins[: plan.inner], ins[plan.inner :]
    plan.line_up(parts, plan.plane_spans(plan.early), y2)
    second = y2[...]
    partial[...] = x[...] + matmul_stacked(wide[...], second)
    product[...] = matmul_nt_pair(second, cotangent_pair[...])


def finish_output(plan, n_in, n_out, *refs):
    me, ins, (output, grad_right_two), (y2, whole) = split_refs(n_in, n_out, refs)
    z, p = me[0] // plan.inner, me[0] % plan.inner
    parts, (partial, product, wide, cotangent_pair) = ins[: plan.inner], ins[plan.inner :]
    spans = plan.plane_spans(plan.late)
    plan.line_up(parts, spans, y2)
    second = y2[...]
    output[...] = partial[...] + matmul_stacked(wide[...], second)
    plan.scatter_rows(product[...], plan.plane_spans(plan.early), whole, z, p)
    plan.scatter_rows(matmul_nt_pair(second, cotangent_pair[...]), spans, whole, z, p)
    grad_right_two[...] = narrow(plan, whole[...]) * plan.factor


def early_input(plan, n_in, n_out, *refs):
    _, ins, (partial, product), (dy1,) = split_refs(n_in, n_out, refs)
    parts, (cotangent, scaled, x_pair, inverse_root) = ins[: len(plan.soon)], ins[len(plan.soon) :]
    plan.line_up(parts, plan.line_spans(plan.soon), dy1)
    back = dy1[...] * inverse_root[...]
    partial[...] = cotangent[...] + matmul_stacked(scaled[...], back)
    product[...] = matmul_nt_pair(back, x_pair[...])


def finish_input(plan, n_in, n_out, *refs):
    me, ins, outs, (dy1, whole, *made, done) = split_refs(n_in, n_out, refs)
    z, p = me[0] // plan.inner, me[0] % plan.inner
    ready, parts, rest = ins[: n_out - len(made)], ins[n_out - len(made) :][: plan.outer], ins[n_out - len(made) + plan.outer :]
    x, x_pair, gain, turned, scaled, inverse_root, partial, product = rest
    stores = [pltpu.make_async_copy(s, t, done.at[i]) for i, (s, t) in enumerate(zip((*ready, *made), outs, strict=True))]
    for store in stores[: len(ready)]:
        store.start()
    input_gradient, gain_gradient, grad_left_one = made
    root = inverse_root[...]
    inner = plan.sums_row(plan.add_sums(parts)) / plan.width
    spans = plan.line_spans(plan.last)
    plan.line_up(parts[: len(plan.last)], spans, dy1)
    back = dy1[...] * root
    input_gradient[...] = partial[...] + matmul_stacked(scaled[...], back) - x[...] * (root * root * inner)
    stores[len(ready)].start()
    plan.scatter_rows(product[...], plan.line_spans(plan.soon), whole, z, p)
    plan.scatter_rows(matmul_nt_pair(back, x_pair[...]), spans, whole, z, p)
    total = whole[...]
    gain_gradient[...] = jnp.sum(turned[...] * total, axis=0, keepdims=True) * plan.factor
    stores[len(ready) + 1].start()
    grad_left_one[...] = (total * gain[...] * plan.factor).T
    stores[len(ready) + 2].start()
    for store in stores:
        store.wait()


def local_tiled(plan, activations, cotangent, gain, left_one, right_one, left_two, right_two):
    features, tokens, count = plan.features, plan.tokens, plan.count
    inner, outer = plan.inner, plan.outer
    me = lax.axis_index("blocks").astype(jnp.int32).reshape(1)
    full, square = (features, tokens), (features, features)
    cost = 12 * features * features * tokens

    def across(messages, step):
        moved = dict(messages)
        for i in messages:
            if i:
                moved[i] = lax.ppermute(messages[i], "blocks", [(s, s ^ (i * step)) for s in range(count)])
        return moved

    def over_outer(keys, messages):
        return across(dict(zip(keys, messages, strict=True)), inner)

    def over_inner(messages):
        return [*across(dict(enumerate(messages)), 1).values()]

    def call(kernel, outs, *args, **options):
        return plan.call(kernel, outs, me, *args, **options)

    gain_row = gain.reshape(1, features)
    one, two = left_one.reshape(square), left_two.reshape(square)
    flat_one, flat_two = right_one.reshape(features, count), right_two.reshape(features, count)

    message, line = plan.message, range(outer)
    early, late, far, near = plan.early, plan.late, plan.far, plan.near

    sent = call(
        first_one, [message(inner, True)] * outer, activations, one, gain_row, scratch=[square], flops=cost, loads=LOADS + 2
    )
    first = over_outer(line, sent)
    *sent, wide_two = call(
        back_two, [message(len(far), False)] * inner + [message(len(near), False)] * inner + [square],
        cotangent, flat_two, scratch=[full], flops=cost,
    )
    dy2_far, dy2_near = over_inner(sent[:inner]), over_inner(sent[inner:])
    half, soon = (features // 2, tokens), features // outer * len(plan.soon)
    stacked_half, stacked_soon, stacked_last = (
        jax.ShapeDtypeStruct((features, 4 * rows), jnp.bfloat16) for rows in (features // 2, soon, features - soon)
    )
    pair = jax.ShapeDtypeStruct((2 * features, tokens), jnp.bfloat16)
    wide_one, turned_one, gain_kept, scaled_early, scaled_late, wide_early, wide_late, x_pair, cotangent_pair = call(
        prepare, [square] * 2 + [(1, features)] + [stacked_soon, stacked_last] + [stacked_half] * 2 + [pair] * 2,
        flat_one, one, gain_row, wide_two, activations, cotangent, scratch=[square], flops=cost // 8,
    )
    sent = call(regroup, [message(len(early), False)] * inner, *(first[k] for k in early), data=len(early))
    first_early = over_inner(sent)
    sent = call(regroup, [message(inner, False)] * len(far), *dy2_far, data=inner)
    dy2_parts = over_outer(far, sent)
    sent = call(regroup, [message(inner, False)] * len(near), *dy2_near, data=inner)
    dy2_parts |= over_outer(near, sent)
    sent = call(regroup, [message(len(late), True)] * inner, *(first[k] for k in (*late, *early)), data=len(late))
    first_late = over_inner(sent)
    *sent, y1, pre, act, slope, inverse_root = call(
        middle, [message(inner, False)] * outer + [full] * 4 + [(1, tokens)], *first_early, *first_late, wide_one, two,
        scratch=[full] * 2, flops=2 * cost,
    )
    second_half = over_outer(line, sent)
    *sent, dy2, dpre = call(
        back_one, [message(len(plan.sooner), True)] * inner + [message(len(plan.later), False)] * inner + [full] * 2,
        *(dy2_parts[k] for k in line), two, wide_one, pre, slope, scratch=[full] * 2, flops=2 * cost,
    )
    dy1_sooner, dy1_later = over_inner(sent[:inner]), over_inner(sent[inner:])
    sent = call(regroup, [message(inner, True)] * len(plan.sooner), *dy1_sooner, data=inner)
    dy1_parts = over_outer(plan.sooner, sent)
    sent = call(regroup, [message(inner, True)] * len(plan.later), *dy1_later, *dy1_sooner, data=inner)
    dy1_parts |= over_outer(plan.later, sent)
    sent = call(regroup, [message(len(early), False)] * inner, *(second_half[k] for k in early), data=len(early))
    second_early = over_inner(sent)
    sent = call(regroup, [message(len(late), False)] * inner, *(second_half[k] for k in late), data=len(late))
    second_late = over_inner(sent)
    grad_right_one, grad_left_two = call(grads_middle, [(features, count), square], y1, dpre, act, dy2, flops=2 * cost)
    partial_output, product_two = call(
        early_output, [full, (features // 2, features)], *second_early, activations, wide_early, cotangent_pair,
        scratch=[half], flops=cost,
    )
    partial_input, product_one = call(
        early_input, [full, (soon, features)], *(dy1_parts[k] for k in plan.soon), cotangent, scaled_early,
        x_pair, inverse_root, scratch=[(soon, tokens)], flops=cost,
    )
    output, grad_right_two = call(
        finish_output, [full, (features, count)], *second_late, partial_output, product_two, wide_late,
        cotangent_pair, scratch=[half, square], flops=cost,
    )
    ready, made = [full, (features, count), square, (features, count)], [full, (1, features), square]
    output, grad_right_one, grad_left_two, grad_right_two, input_gradient, gain_gradient, grad_left_one = call(
        finish_input, ready + made, output, grad_right_one, grad_left_two, grad_right_two,
        *(dy1_parts[k] for k in (*plan.last, *plan.soon)), activations, x_pair, gain_kept, turned_one, scaled_late, inverse_root,
        partial_input, product_one, scratch=[(features - soon, tokens), square, *made], flops=cost, stores=len(ready + made),
    )
    return (
        output,
        input_gradient,
        gain_gradient.reshape(features),
        grad_left_one.reshape(left_one.shape),
        grad_right_one.reshape(right_one.shape),
        grad_left_two.reshape(left_two.shape),
        grad_right_two.reshape(right_two.shape),
    )


def local(activations, *rest):
    plan = Plan(lax.axis_size("blocks"), *activations.shape)
    if plan.fits() and rest[2].shape[0] == 1:
        return local_tiled(plan, activations, *rest)
    return local_plain(activations, *rest)


def solution(mesh):
    split = P("blocks", "groups")
    kept, laid = P("blocks", None, None), P(("groups", "blocks"), None, None)
    return jax.shard_map(
        local,
        mesh=mesh,
        in_specs=(split, split, P("blocks"), kept, kept, kept, kept),
        out_specs=(split, split, P(("groups", "blocks")), laid, laid, laid, laid),
        check_vma=False,
    )
```
